256 devices in a mesh: row: 64 (over z_hi, y, x), rep: 4 (over z_lo, core).
Axes of the slice: x: 4, y: 4, z: 8 (z_hi: 4, z_lo: 2; z = z_hi * 2 + z_lo), core: 2. Of those that a mesh axis runs over, the one named last changes fastest.
Arguments:
- features: bfloat16 [32768, 128], P('row'), may hold values from -6 to 6
- weight_one: bfloat16 [128, 128], replicated, may hold values from -0.5 to 0.5
- weight_two: bfloat16 [128, 128], replicated, may hold values from -0.5 to 0.5
- cotangent: bfloat16 [32768, 128], P('row'), may hold values from -0.03125 to 0.03125
- adj_tiles: bfloat16 [64, 64, 16, 128, 128], P('row', 'rep'), may hold values from -0.09375 to 0.09375
- tile_rows: int32 [64, 64, 16], P('row', 'rep'), may hold values from 0 to 3, as said below
- tile_cols: int32 [64, 64, 16], P('row', 'rep'), may hold values from 0 to 3
- tile_counts: int32 [64, 64], P('row', 'rep'), may hold values from 0 to 16, as said below
Outputs:
- output: bfloat16 [32768, 128], P('row')
- grad_one: float32 [128, 128], replicated
- grad_two: float32 [128, 128], replicated
The draws below stay inside these ranges and needn't reach their ends.
Inputs may be any that keep to these rules, and one draw needn't show every extreme that they name: Only slots 0 to tile_counts[b, s] - 1 of block-row b and section s are live; the other slots carry arbitrary tiles and indices that are not part of A. Section b of block-row b holds 16 live slots; many other sections hold none. `tile_rows`: the (row, column) pairs of the slots of one block-row and section are distinct.
All inputs are finite; a program needn't handle non-finite values.
Results may differ from the reference program's by a relative error of at most 0.0065.
Values may be sent and summed in bfloat16 or wider, within the bound.
A program may use at most 192 MiB of HBM per device.

```python
import jax
import jax.numpy as jnp
from jax import lax

F = 128
TILE = 128
NB = 512
MOST = 16
NBLK = 64
SECTIONS = 64
NODES = 32768
N_ROW = 64


def tile_layout(key):
    layout_key = jax.random.fold_in(key, 7)
    count_tiles = NB // TILE
    cell_total = count_tiles * count_tiles
    slot_keys = jax.random.split(layout_key, NBLK * SECTIONS)
    orders = jax.vmap(lambda one_key: jax.random.permutation(one_key, cell_total))(slot_keys)
    chosen = orders[:, :MOST].reshape(NBLK, SECTIONS, MOST).astype(jnp.int32)
    return ((chosen // count_tiles).astype(jnp.int32), (chosen % count_tiles).astype(jnp.int32))


def draw_tile_rows(key, part):
    return tile_layout(key)[0]


def draw_tile_cols(key, part):
    return tile_layout(key)[1]


def draw_tile_counts(key, part):
    count_key = jax.random.fold_in(key, 11)
    first_key, second_key, factor_key = jax.random.split(count_key, 3)
    first = jax.random.randint(first_key, (NBLK, SECTIONS), 0, 4)
    second = jax.random.randint(second_key, (NBLK, SECTIONS), 0, 4)
    factor = jax.random.randint(factor_key, (NBLK, 1), 2, 6)
    counts = jnp.minimum(MOST, first * second * factor // 4)
    diagonal = jnp.arange(NBLK)[:, None] == jnp.arange(SECTIONS)[None, :]
    return jnp.where(diagonal, MOST, counts).astype(jnp.int32)


def steps_of(rng, shape, pieces, smallest, largest):
    gain = 1.0
    for axis_at, blocks in pieces:
        heights = jax.random.uniform(jax.random.fold_in(jax.random.fold_in(rng, 6), axis_at), (blocks,), jnp.float32, smallest / len(pieces), largest / len(pieces))
        gain = gain * jnp.repeat(jnp.exp(heights), shape[axis_at] // blocks).reshape((-1,) + (1,) * (len(shape) - 1 - axis_at))
    return gain


def scatter_about(key, dims, scale, most, pieces=(), kind=jnp.bfloat16):
    entries = jax.random.normal(key, dims, jnp.float32) * scale
    if len(pieces) > 0:
        entries = steps_of(key, dims, pieces, -0.22, 0.18) * entries
    return jnp.clip(entries, min=-most, max=most).astype(kind)


def setup_inputs(seed: int = 0) -> dict:
    keys = jax.random.split(jax.random.key(seed), 9)
    return {
        "features": scatter_about(keys[0], (NODES, F), 1.0, 6.0, ((0, 64),)),
        "weight_one": scatter_about(keys[1], (F, F), F ** -0.5, 0.5),
        "weight_two": scatter_about(keys[2], (F, F), F ** -0.5, 0.5),
        "cotangent": scatter_about(keys[3], (NODES, F), (NODES ** -0.5), 0.03125, ((0, 64),)),
        "adj_tiles": scatter_about(keys[4], (NBLK, SECTIONS, MOST, TILE, TILE), ((TILE * TILE * (MOST + 2 * N_ROW) // NB) ** -0.5), 0.09375, ((0, 64), (1, 4))),
        "tile_rows": draw_tile_rows(jax.random.fold_in(keys[8], 71), 0),
        "tile_cols": draw_tile_cols(jax.random.fold_in(keys[8], 71), 0),
        "tile_counts": draw_tile_counts(jax.random.fold_in(keys[8], 71), 0),
    }


def gelu_value(values):
    return values * 0.5 * (1.0 + lax.erf(values * 0.7071067811865476))


def gelu_slope(values):
    normal_cdf = 0.5 * (1.0 + lax.erf(values * 0.7071067811865476))
    return normal_cdf + values * jnp.exp(-0.5 * values * values) * 0.3989422804014327


def row_contract(left, right):
    return lax.dot_general(left, right, (((0,), (0,)), ((), ())), preferred_element_type=jnp.float32)


def propagate(adj_tiles, tile_rows, tile_cols, tile_counts, node_values):
    count_tiles = NB // TILE
    blocks = node_values.reshape(SECTIONS, count_tiles, TILE, F)
    section_ids = jnp.arange(SECTIONS, dtype=jnp.int32)[:, None]

    def one_block_row(inputs):
        tile_data, row_ids, col_ids, live_counts = inputs
        sources = blocks[section_ids, col_ids]
        products = jnp.einsum("smij,smjf->smif", tile_data.astype(jnp.float32), sources.astype(jnp.float32),
                              precision=lax.Precision.HIGHEST)
        live_mask = jnp.arange(MOST, dtype=jnp.int32)[None, :] < live_counts[:, None]
        onehot = jnp.where(live_mask[..., None] & (row_ids[..., None] == jnp.arange(count_tiles, dtype=jnp.int32)),
                           1.0, 0.0).astype(jnp.float32)
        summed = jnp.einsum("smk,smif->kif", onehot, products, precision=lax.Precision.HIGHEST)
        return summed.reshape(NB, F)

    return lax.map(one_block_row, (adj_tiles, tile_rows, tile_cols, tile_counts)).reshape(NODES, F)


def reference(features, weight_one, weight_two, cotangent, adj_tiles, tile_rows, tile_cols, tile_counts):
    s_one = propagate(adj_tiles, tile_rows, tile_cols, tile_counts, features).astype(jnp.bfloat16)
    pre_one = jnp.dot(s_one, weight_one, preferred_element_type=jnp.float32)
    hidden = gelu_value(pre_one).astype(jnp.bfloat16)
    s_two = propagate(adj_tiles, tile_rows, tile_cols, tile_counts, hidden).astype(jnp.bfloat16)
    output = jnp.dot(s_two, weight_two, preferred_element_type=jnp.float32).astype(jnp.bfloat16)
    grad_two = row_contract(s_two, cotangent)
    d_two = lax.dot_general(cotangent, weight_two, (((1,), (1,)), ((), ())),
                            preferred_element_type=jnp.float32).astype(jnp.bfloat16)
    d_hidden = propagate(adj_tiles, tile_rows, tile_cols, tile_counts, d_two)
    d_pre = (d_hidden * gelu_slope(pre_one)).astype(jnp.bfloat16)
    grad_one = row_contract(s_one, d_pre)
    return output, grad_one, grad_two
```

```python
import jax
import jax.numpy as jnp
from jax import lax
from jax.experimental import pallas as pl
from jax.experimental.pallas import tpu as pltpu
from jax.sharding import PartitionSpec as P

MESH = pl.DeviceIdType.MESH
TILE = 128
NB = 512
HALF = 256
SIDE = 4
PLANE = 16
REPS = 4
DEAD = 256
BF16 = jnp.bfloat16
F32 = jnp.float32


def gelu_parts(values):
    normal_cdf = 0.5 * (1.0 + lax.erf(values * 0.7071067811865476))
    slope = normal_cdf + values * jnp.exp(-0.5 * values * values) * 0.3989422804014327
    return values * normal_cdf, slope


def wrap(value, size):
    return lax.rem(value + size, size)


def ring_step(index):
    return index + index // 2 - 2 * (index // 3)


def step_kernel(
    feat, w_one, w_two, cot, adj, rows_in, cols_in, counts_in,
    out, grad_one, grad_two,
    tiles, table_v, table_s, xf, xd, xh, dq, hq, acc_f, acc_d, acc_h,
    part_f, part_d, part_h, red_f, red_d, red_h, s_one_q, slope_q, out_buf,
    gpart, grs, gcol, gred, gall,
    local_sem, z_send, z_recv, a_send, a_recv, b_send, b_recv,
    r_send, r_recv, o_send, o_recv, g_send, g_recv,
):
    row = lax.axis_index("row")
    rep = lax.axis_index("rep")
    zh = row // PLANE
    place = lax.rem(row, PLANE)
    y = place // SIDE
    x = lax.rem(place, SIDE)
    column = zh * REPS + rep

    adj_copy = pltpu.make_async_copy(adj, tiles.at[pl.ds(0, DEAD)], local_sem.at[0])
    adj_copy.start()

    def plane_peer(step):
        return (zh * PLANE + wrap(place + step, PLANE), rep)

    def column_peer(step):
        other = wrap(column + step, PLANE)
        return ((other // REPS) * PLANE + place, lax.rem(other, REPS))

    def rep_peer(step):
        return (row, wrap(rep + step, REPS))

    def x_peer(step):
        return (zh * PLANE + y * SIDE + wrap(x + step, SIDE), rep)

    def y_peer(step):
        return (zh * PLANE + wrap(y + step, SIDE) * SIDE + x, rep)

    def remote(src, dst, send, recv, peer):
        return pltpu.make_async_remote_copy(
            src_ref=src, dst_ref=dst, send_sem=send, recv_sem=recv,
            device_id=peer, device_id_type=MESH,
        )

    barrier = pltpu.get_barrier_semaphore()

    def greet(step, carry):
        pl.semaphore_signal(barrier, inc=1, device_id=plane_peer(step), device_id_type=MESH)
        pl.semaphore_signal(barrier, inc=1, device_id=column_peer(step), device_id_type=MESH)
        return carry

    lax.fori_loop(1, PLANE, greet, 0)
    pl.semaphore_wait(barrier, 2 * (PLANE - 1))

    def z_copy(t, buf, src, step):
        return remote(
            src,
            buf.at[place, pl.ds(pl.multiple_of(rep * TILE, TILE), TILE)],
            z_send.at[t, step], z_recv.at[t, rep],
            (wrap(zh + step, REPS) * PLANE + place, zh),
        )

    def z_start(t, buf, src):
        for step in (1, 2, 3):
            z_copy(t, buf, src, step).start()

        @pl.when(rep != zh)
        def _():
            z_copy(t, buf, src, 0).start()

        @pl.when(rep == zh)
        def _():
            buf[place, pl.ds(pl.multiple_of(rep * TILE, TILE), TILE)] = src[...]

    def z_finish(t, buf, src):
        for step in (1, 2, 3):
            z_copy(t, buf, src, step).wait_send()

        @pl.when(rep != zh)
        def _():
            z_copy(t, buf, src, 0).wait_send()

    def z_wait(t, buf, src, quarter):
        @pl.when(jnp.logical_or(rep != zh, rep != quarter))
        def _():
            remote(
                src, buf.at[place, pl.ds(quarter * TILE, TILE)],
                z_send.at[t, 0], z_recv.at[t, quarter], rep_peer(1),
            ).wait_recv()

    def a_block(dy, dx):
        return wrap(y - dy, SIDE) * SIDE + wrap(x - dx, SIDE)

    def half_a(buf, block):
        return buf.at[block, pl.ds(0, HALF)]

    def half_b(buf, block):
        return buf.at[block, pl.ds(HALF, HALF)]

    def first_a(t, buf, i, block):
        return remote(half_a(buf, block), half_a(buf, block),
                      a_send.at[t, i], a_recv.at[t, i], x_peer(ring_step(i + 1)))

    def first_b(t, buf, i, block):
        return remote(half_b(buf, block), half_b(buf, block),
                      b_send.at[t, i], b_recv.at[t, i], y_peer(ring_step(i + 1)))

    def second_a(t, buf, j, i, block):
        return remote(half_a(buf, block), half_a(buf, block),
                      a_send.at[t, 3 + 4 * j + i], a_recv.at[t, 3 + 4 * j + i],
                      y_peer(ring_step(j + 1)))

    def second_b(t, buf, j, i, block):
        return remote(half_b(buf, block), half_b(buf, block),
                      b_send.at[t, 3 + 4 * j + i], b_recv.at[t, 3 + 4 * j + i],
                      x_peer(ring_step(j + 1)))

    def spread_start(t, buf, src):
        z_wait(t, buf, src, 0)
        z_wait(t, buf, src, 1)
        for i in range(3):
            first_a(t, buf, i, place).start()
        z_wait(t, buf, src, 2)
        z_wait(t, buf, src, 3)
        for i in range(3):
            first_b(t, buf, i, place).start()
        for j in range(3):
            second_a(t, buf, j, 0, place).start()
            second_b(t, buf, j, 0, place).start()

    def spread_forward(t, buf):
        def body(i, carry):
            away = ring_step(i + 1)
            from_x = a_block(0, away)
            first_a(t, buf, i, from_x).wait_recv()
            for j in range(3):
                second_a(t, buf, j, i + 1, from_x).start()
            from_y = a_block(away, 0)
            first_b(t, buf, i, from_y).wait_recv()
            for j in range(3):
                second_b(t, buf, j, i + 1, from_y).start()
            return carry

        lax.fori_loop(0, 3, body, 0)

    def spread_finish(t, buf):
        def body(i, carry):
            first_a(t, buf, i, place).wait_send()
            first_b(t, buf, i, place).wait_send()
            for j in range(4):
                second_a(t, buf, i, j, place).wait_send()
                second_b(t, buf, i, j, place).wait_send()
            return carry

        lax.fori_loop(0, 3, body, 0)

    def consume(buf, acc, block, half):
        right = buf[block, pl.ds(half * HALF, HALF)]
        for k in range(4):
            left = jnp.concatenate(
                [tiles[table_s[block, 4 * k + 2 * half]], tiles[table_s[block, 4 * k + 2 * half + 1]]],
                axis=1,
            )
            acc[pl.ds(k * TILE, TILE)] += jnp.dot(left, right, preferred_element_type=F32)

    def consume_near(buf, acc):
        def body(i, carry):
            away = ring_step(i)
            consume(buf, acc, a_block(0, away), 0)
            consume(buf, acc, a_block(away, 0), 1)
            return carry

        lax.fori_loop(0, 4, body, 0)

    def consume_far(t, buf, acc, start, stop):
        def body(n, carry):
            j = n // 4
            i = lax.rem(n, 4)
            e = ring_step(j + 1)
            d = ring_step(i)
            block = a_block(e, d)
            second_a(t, buf, j, i, block).wait_recv()
            consume(buf, acc, block, 0)
            block = a_block(d, e)
            second_b(t, buf, j, i, block).wait_recv()
            consume(buf, acc, block, 1)
            return carry

        lax.fori_loop(start, stop, body, 0)

    def rep_copy(t, part, red, step):
        return remote(
            part.at[pl.ds(pl.multiple_of(wrap(rep + step, REPS) * TILE, TILE), TILE)],
            red.at[step - 1], r_send.at[t, step - 1], r_recv.at[t, step - 1],
            rep_peer(step),
        )

    def rep_start(t, acc, part, red):
        part[...] = acc[...].astype(BF16)
        for step in (2, 3, 1):
            rep_copy(t, part, red, step).start()

    def rep_sum(t, acc, part, red):
        total = acc[pl.ds(pl.multiple_of(rep * TILE, TILE), TILE)]
        for step in (1, 2, 3):
            rep_copy(t, part, red, step).wait_recv()
            total = total + red[step - 1].astype(F32)
        return total

    quarter = pl.ds(pl.multiple_of(rep * TILE, TILE), TILE)

    fq = feat.at[quarter]
    z_start(0, xf, fq)
    dq[...] = lax.dot_general(
        cot[quarter], w_two[...], (((1,), (1,)), ((), ())), preferred_element_type=F32
    ).astype(BF16)
    z_start(1, xd, dq)

    lanes = lax.broadcasted_iota(jnp.int32, (PLANE, TILE), 1)
    sections = lax.broadcasted_iota(jnp.int32, (PLANE, TILE), 0)
    small_lane = lax.broadcasted_iota(jnp.int32, (PLANE, PLANE), 1)
    small_row = lax.broadcasted_iota(jnp.int32, (PLANE, PLANE), 0)
    count_wide = jnp.broadcast_to(counts_in[...].astype(F32), (PLANE, PLANE))
    count_col = jnp.sum(jnp.where(small_lane == small_row, count_wide, 0.0), axis=1, keepdims=True)
    cell = jnp.where(
        small_lane.astype(F32) < count_col, rows_in[...] * 4 + cols_in[...], -1
    )
    table = jnp.full((PLANE, TILE), DEAD, jnp.int32)
    for slot in range(16):
        table = jnp.where(cell[:, slot : slot + 1] == lanes, sections * 16 + slot, table)
    table_v[...] = table
    table_copy = pltpu.make_async_copy(table_v, table_s, local_sem.at[1])
    table_copy.start()
    tiles[DEAD] = jnp.zeros((TILE, TILE), BF16)
    acc_f[...] = jnp.zeros_like(acc_f)
    acc_d[...] = jnp.zeros_like(acc_d)
    acc_h[...] = jnp.zeros_like(acc_h)

    spread_start(0, xf, fq)
    table_copy.wait()
    adj_copy.wait()
    spread_forward(0, xf)
    consume_near(xf, acc_f)
    spread_start(1, xd, dq)
    consume_far(0, xf, acc_f, 0, 12)
    rep_start(0, acc_f, part_f, red_f)
    spread_forward(1, xd)

    s_one = rep_sum(0, acc_f, part_f, red_f).astype(BF16)
    pre_one = jnp.dot(s_one, w_one[...], preferred_element_type=F32)
    hidden, slope = gelu_parts(pre_one)
    hq[...] = hidden.astype(BF16)
    z_start(2, xh, hq)
    s_one_q[...] = s_one
    slope_q[...] = slope
    consume_near(xd, acc_d)
    spread_start(2, xh, hq)
    consume_far(1, xd, acc_d, 0, 12)
    rep_start(1, acc_d, part_d, red_d)
    spread_forward(2, xh)
    consume_near(xh, acc_h)
    d_pre = (rep_sum(1, acc_d, part_d, red_d) * slope_q[...]).astype(BF16)
    g_one = lax.dot_general(
        s_one_q[...], d_pre, (((0,), (0,)), ((), ())), preferred_element_type=F32
    )
    gpart[:, 0:8, :] = g_one.reshape(PLANE, 8, TILE)
    consume_far(2, xh, acc_h, 0, 12)
    rep_start(2, acc_h, part_h, red_h)

    g_two = lax.dot_general(
        part_h[...], cot[...], (((0,), (0,)), ((), ())), preferred_element_type=F32
    )
    gpart[:, 8:16, :] = g_two.reshape(PLANE, 8, TILE)

    def plane_sum(step):
        return remote(
            gpart.at[wrap(place + step, PLANE)], grs.at[step],
            g_send.at[0, step], g_recv.at[0, step], plane_peer(step),
        )

    def column_share(step):
        return remote(
            gcol.at[column], gcol.at[column],
            g_send.at[1, step], g_recv.at[1, step], column_peer(step),
        )

    def plane_gather(step):
        return remote(
            gred, gall.at[place],
            g_send.at[2, step], g_recv.at[2, step], plane_peer(step),
        )

    def start_all(make):
        def body(step, carry):
            make(step).start()
            return carry

        lax.fori_loop(1, PLANE, body, 0)

    def receive_all(make):
        def body(step, carry):
            make(step).wait_recv()
            return carry

        lax.fori_loop(1, PLANE, body, 0)

    def sent_all(make):
        def body(step, carry):
            make(step).wait_send()
            return carry

        lax.fori_loop(1, PLANE, body, 0)

    start_all(plane_sum)

    s_two = rep_sum(2, acc_h, part_h, red_h).astype(BF16)
    out_buf[quarter] = jnp.dot(s_two, w_two[...], preferred_element_type=F32).astype(BF16)

    def out_copy(step):
        return remote(
            out_buf.at[quarter], out_buf.at[quarter],
            o_send.at[step - 1], o_recv.at[step - 1], rep_peer(step),
        )

    for step in (2, 3, 1):
        out_copy(step).start()

    receive_all(plane_sum)
    mine = gpart[place]
    for step in range(1, PLANE):
        mine = mine + grs[step]
    gcol[column] = mine
    start_all(column_share)
    receive_all(column_share)
    mine = gcol[0]
    for other in range(1, PLANE):
        mine = mine + gcol[other]
    gred[...] = mine
    start_all(plane_gather)
    gall[place] = mine

    for step in (1, 2, 3):
        out_copy(step).wait_recv()
    out[...] = out_buf[...]
    receive_all(plane_gather)
    grad_one[...] = gall[:, 0:8, :].reshape(TILE, TILE)
    grad_two[...] = gall[:, 8:16, :].reshape(TILE, TILE)

    for t, buf, src in ((0, xf, fq), (1, xd, dq), (2, xh, hq)):
        z_finish(t, buf, src)
        spread_finish(t, buf)
    for t, part, red in ((0, part_f, red_f), (1, part_d, red_d), (2, part_h, red_h)):
        for step in (1, 2, 3):
            rep_copy(t, part, red, step).wait_send()
    for step in (1, 2, 3):
        out_copy(step).wait_send()
    sent_all(plane_sum)
    sent_all(column_share)
    sent_all(plane_gather)


def per_device(
    features, weight_one, weight_two, cotangent, adj_tiles, tile_rows, tile_cols, tile_counts
):
    vmem = pl.BlockSpec(memory_space=pltpu.VMEM)
    dma = pltpu.SemaphoreType.DMA
    return pl.pallas_call(
        step_kernel,
        name="graph_step",
        out_shape=(
            jax.ShapeDtypeStruct((NB, TILE), BF16),
            jax.ShapeDtypeStruct((TILE, TILE), F32),
            jax.ShapeDtypeStruct((TILE, TILE), F32),
        ),
        in_specs=[vmem, vmem, vmem, vmem, pl.BlockSpec(memory_space=pl.ANY), vmem, vmem, vmem],
        out_specs=(vmem, vmem, vmem),
        scratch_shapes=[
            pltpu.VMEM((DEAD + 1, TILE, TILE), BF16),
            pltpu.VMEM((PLANE, TILE), jnp.int32),
            pltpu.SMEM((PLANE, TILE), jnp.int32),
            pltpu.VMEM((PLANE, NB, TILE), BF16),
            pltpu.VMEM((PLANE, NB, TILE), BF16),
            pltpu.VMEM((PLANE, NB, TILE), BF16),
            pltpu.VMEM((TILE, TILE), BF16),
            pltpu.VMEM((TILE, TILE), BF16),
            pltpu.VMEM((NB, TILE), F32),
            pltpu.VMEM((NB, TILE), F32),
            pltpu.VMEM((NB, TILE), F32),
            pltpu.VMEM((NB, TILE), BF16),
            pltpu.VMEM((NB, TILE), BF16),
            pltpu.VMEM((NB, TILE), BF16),
            pltpu.VMEM((3, TILE, TILE), BF16),
            pltpu.VMEM((3, TILE, TILE), BF16),
            pltpu.VMEM((3, TILE, TILE), BF16),
            pltpu.VMEM((TILE, TILE), BF16),
            pltpu.VMEM((TILE, TILE), F32),
            pltpu.VMEM((NB, TILE), BF16),
            pltpu.VMEM((PLANE, 16, TILE), F32),
            pltpu.VMEM((PLANE, 16, TILE), F32),
            pltpu.VMEM((PLANE, 16, TILE), F32),
            pltpu.VMEM((16, TILE), F32),
            pltpu.VMEM((PLANE, 16, TILE), F32),
            dma((2,)),
            dma((3, 4)),
            dma((3, 4)),
            dma((3, 15)),
            dma((3, 15)),
            dma((3, 15)),
            dma((3, 15)),
            dma((3, 3)),
            dma((3, 3)),
            dma((3,)),
            dma((3,)),
            dma((3, 16)),
            dma((3, 16)),
        ],
        compiler_params=pltpu.CompilerParams(
            collective_id=0, has_side_effects=True, vmem_limit_bytes=48 << 20
        ),
    )(
        features, weight_one, weight_two, cotangent,
        adj_tiles.reshape(DEAD, TILE, TILE),
        tile_rows.reshape(PLANE, 16), tile_cols.reshape(PLANE, 16), tile_counts,
    )


def solution(mesh):
    placed = (
        P("row", None),
        P(),
        P(),
        P("row", None),
        P("row", "rep", None, None, None),
        P("row", "rep", None),
        P("row", "rep", None),
        P("row", "rep"),
    )
    return jax.shard_map(
        per_device,
        mesh=mesh,
        in_specs=placed,
        out_specs=(P("row", None), P(), P()),
        check_vma=False,
    )
```

```python
import jax
import jax.numpy as jnp
from jax import lax
from jax.experimental import pallas as pl
from jax.experimental.pallas import tpu as pltpu
from jax.sharding import PartitionSpec as P

MESH = pl.DeviceIdType.MESH
TILE = 128
NB = 512
HALF = 256
SIDE = 4
PLANE = 16
REPS = 4
DEAD = 256
BF16 = jnp.bfloat16
F32 = jnp.float32


def gelu_parts(values):
    normal_cdf = 0.5 * (1.0 + lax.erf(values * 0.7071067811865476))
    slope = normal_cdf + values * jnp.exp(-0.5 * values * values) * 0.3989422804014327
    return values * normal_cdf, slope


def wrap(value, size):
    return lax.rem(value + size, size)


def ring_step(index):
    return index + index // 2 - 2 * (index // 3)


def step_kernel(
    feat, w_one_in, w_two_in, cot_in, adj, rows_hbm, cols_hbm, counts_hbm,
    out, grad_one, grad_two,
    w_one, w_two, cot, rows_in, cols_in, counts_in, tiles, table_v, table_s, xf, xd, xh, dq, hq, acc_f, acc_d, acc_h,
    part_f, part_d, part_h, red_f, red_d, red_h, s_one_q, slope_q, out_buf,
    gpart, grs, gcol, gred, gall,
    local_sem, z_send, z_recv, a_send, a_recv, b_send, b_recv,
    r_send, r_recv, o_send, o_recv, g_send, g_recv,
):
    row = lax.axis_index("row")
    rep = lax.axis_index("rep")
    zh = row // PLANE
    place = lax.rem(row, PLANE)
    y = place // SIDE
    x = lax.rem(place, SIDE)
    column = zh * REPS + rep


    def plane_peer(step):
        return (zh * PLANE + wrap(place + step, PLANE), rep)

    def column_peer(step):
        other = wrap(column + step, PLANE)
        return ((other // REPS) * PLANE + place, lax.rem(other, REPS))

    def rep_peer(step):
        return (row, wrap(rep + step, REPS))

    def x_peer(step):
        return (zh * PLANE + y * SIDE + wrap(x + step, SIDE), rep)

    def y_peer(step):
        return (zh * PLANE + wrap(y + step, SIDE) * SIDE + x, rep)

    def remote(src, dst, send, recv, peer):
        return pltpu.make_async_remote_copy(
            src_ref=src, dst_ref=dst, send_sem=send, recv_sem=recv,
            device_id=peer, device_id_type=MESH,
        )

    def local(src, dst, at):
        return pltpu.make_async_copy(src, dst, local_sem.at[at])

    barrier = pltpu.get_barrier_semaphore()

    def greet(peer):
        pl.semaphore_signal(barrier, inc=1, device_id=peer, device_id_type=MESH)

    for q in range(REPS):
        @pl.when(jnp.logical_or(rep != zh, rep != q))
        def _(q=q):
            greet((rep * PLANE + place, q))

    for step in (2, 1, 3):
        greet(x_peer(step))
        greet(y_peer(step))
        greet(rep_peer(step))
    loads = [
        local(cot_in, cot, 0), local(w_two_in, w_two, 1), local(counts_hbm, counts_in, 2),
        local(rows_hbm, rows_in, 3), local(cols_hbm, cols_in, 4), local(w_one_in, w_one, 5),
        local(adj, tiles.at[pl.ds(0, DEAD)], 6),
    ]
    for load in loads:
        load.start()
    pl.semaphore_wait(barrier, 13 - jnp.where(rep == zh, 1, 0))

    def z_copy(t, buf, src, step):
        return remote(
            src,
            buf.at[place, pl.ds(pl.multiple_of(rep * TILE, TILE), TILE)],
            z_send.at[t, step], z_recv.at[t, rep],
            (wrap(zh + step, REPS) * PLANE + place, zh),
        )

    def own_copy(t, buf, src):
        return local(src, buf.at[place, pl.ds(pl.multiple_of(rep * TILE, TILE), TILE)], 8 + t)

    def z_start(t, buf, src):
        for step in (2, 1, 3):
            z_copy(t, buf, src, step).start()

        @pl.when(rep != zh)
        def _():
            z_copy(t, buf, src, 0).start()

        @pl.when(rep == zh)
        def _():
            own_copy(t, buf, src).start()

    def z_finish(t, buf, src):
        for step in (1, 2, 3):
            z_copy(t, buf, src, step).wait_send()

        @pl.when(rep != zh)
        def _():
            z_copy(t, buf, src, 0).wait_send()

    def z_wait(t, buf, src, quarter):
        @pl.when(jnp.logical_or(rep != zh, rep != quarter))
        def _():
            remote(
                src, buf.at[place, pl.ds(quarter * TILE, TILE)],
                z_send.at[t, 0], z_recv.at[t, quarter], rep_peer(1),
            ).wait_recv()

        @pl.when(jnp.logical_and(rep == zh, rep == quarter))
        def _():
            own_copy(t, buf, src).wait()

    def a_block(dy, dx):
        return wrap(y - dy, SIDE) * SIDE + wrap(x - dx, SIDE)

    def half_a(buf, block):
        return buf.at[block, pl.ds(0, HALF)]

    def half_b(buf, block):
        return buf.at[block, pl.ds(HALF, HALF)]

    def first_a(t, buf, i, block):
        return remote(half_a(buf, block), half_a(buf, block),
                      a_send.at[t, i], a_recv.at[t, i], x_peer(ring_step(i + 1)))

    def first_b(t, buf, i, block):
        return remote(half_b(buf, block), half_b(buf, block),
                      b_send.at[t, i], b_recv.at[t, i], y_peer(ring_step(i + 1)))

    def second_a(t, buf, j, i, block):
        return remote(half_a(buf, block), half_a(buf, block),
                      a_send.at[t, 3 + 4 * j + i], a_recv.at[t, 3 + 4 * j + i],
                      y_peer(ring_step(j + 1)))

    def second_b(t, buf, j, i, block):
        return remote(half_b(buf, block), half_b(buf, block),
                      b_send.at[t, 3 + 4 * j + i], b_recv.at[t, 3 + 4 * j + i],
                      x_peer(ring_step(j + 1)))

    def spread_start(t, buf, src):
        z_wait(t, buf, src, 0)
        z_wait(t, buf, src, 1)
        for i in range(3):
            first_a(t, buf, i, place).start()
        z_wait(t, buf, src, 2)
        z_wait(t, buf, src, 3)
        for i in range(3):
            first_b(t, buf, i, place).start()
        for j in range(3):
            second_a(t, buf, j, 0, place).start()
            second_b(t, buf, j, 0, place).start()

    def spread_forward(t, buf):
        def body(i, carry):
            away = ring_step(i + 1)
            from_x = a_block(0, away)
            first_a(t, buf, i, from_x).wait_recv()
            for j in range(3):
                second_a(t, buf, j, i + 1, from_x).start()
            from_y = a_block(away, 0)
            first_b(t, buf, i, from_y).wait_recv()
            for j in range(3):
                second_b(t, buf, j, i + 1, from_y).start()
            return carry

        lax.fori_loop(0, 3, body, 0)

    def spread_finish(t, buf):
        def body(i, carry):
            first_a(t, buf, i, place).wait_send()
            first_b(t, buf, i, place).wait_send()
            for j in range(4):
                second_a(t, buf, i, j, place).wait_send()
                second_b(t, buf, i, j, place).wait_send()
            return carry

        lax.fori_loop(0, 3, body, 0)

    def consume(buf, acc, block, half):
        right = buf[block, pl.ds(half * HALF, HALF)]
        for k in range(4):
            left = jnp.concatenate(
                [tiles[table_s[block, 4 * k + 2 * half]], tiles[table_s[block, 4 * k + 2 * half + 1]]],
                axis=1,
            )
            acc[pl.ds(k * TILE, TILE)] += jnp.dot(left, right, preferred_element_type=F32)

    def consume_near(buf, acc):
        def body(i, carry):
            away = ring_step(i)
            consume(buf, acc, a_block(0, away), 0)
            consume(buf, acc, a_block(away, 0), 1)
            return carry

        lax.fori_loop(0, 4, body, 0)

    def consume_far(t, buf, acc, start, stop):
        def body(n, carry):
            j = n // 4
            i = lax.rem(n, 4)
            e = ring_step(j + 1)
            d = ring_step(i)
            block = a_block(e, d)
            second_a(t, buf, j, i, block).wait_recv()
            consume(buf, acc, block, 0)
            block = a_block(d, e)
            second_b(t, buf, j, i, block).wait_recv()
            consume(buf, acc, block, 1)
            return carry

        lax.fori_loop(start, stop, body, 0)

    def rep_copy(t, part, red, step):
        return remote(
            part.at[pl.ds(pl.multiple_of(wrap(rep + step, REPS) * TILE, TILE), TILE)],
            red.at[step - 1], r_send.at[t, step - 1], r_recv.at[t, step - 1],
            rep_peer(step),
        )

    def rep_start(t, acc, part, red):
        part[...] = acc[...].astype(BF16)
        for step in (2, 3, 1):
            rep_copy(t, part, red, step).start()

    def rep_sum(t, acc, part, red):
        total = acc[pl.ds(pl.multiple_of(rep * TILE, TILE), TILE)]
        for step in (1, 2, 3):
            rep_copy(t, part, red, step).wait_recv()
            total = total + red[step - 1].astype(F32)
        return total

    quarter = pl.ds(pl.multiple_of(rep * TILE, TILE), TILE)

    fq = feat.at[quarter]
    z_start(0, xf, fq)
    loads[0].wait()
    loads[1].wait()
    dq[...] = lax.dot_general(
        cot[quarter], w_two[...], (((1,), (1,)), ((), ())), preferred_element_type=F32
    ).astype(BF16)
    z_start(1, xd, dq)

    loads[2].wait()
    loads[3].wait()
    loads[4].wait()
    lanes = lax.broadcasted_iota(jnp.int32, (PLANE, TILE), 1)
    sections = lax.broadcasted_iota(jnp.int32, (PLANE, TILE), 0)
    small_lane = lax.broadcasted_iota(jnp.int32, (PLANE, PLANE), 1)
    small_row = lax.broadcasted_iota(jnp.int32, (PLANE, PLANE), 0)
    count_wide = jnp.broadcast_to(counts_in[...].astype(F32), (PLANE, PLANE))
    count_col = jnp.sum(jnp.where(small_lane == small_row, count_wide, 0.0), axis=1, keepdims=True)
    cell = jnp.where(
        small_lane.astype(F32) < count_col, rows_in[...] * 4 + cols_in[...], -1
    )
    table = jnp.full((PLANE, TILE), DEAD, jnp.int32)
    for slot in range(16):
        table = jnp.where(cell[:, slot : slot + 1] == lanes, sections * 16 + slot, table)
    table_v[...] = table
    table_copy = local(table_v, table_s, 7)
    table_copy.start()
    tiles[DEAD] = jnp.zeros((TILE, TILE), BF16)
    acc_f[...] = jnp.zeros_like(acc_f)
    acc_d[...] = jnp.zeros_like(acc_d)
    acc_h[...] = jnp.zeros_like(acc_h)

    spread_start(0, xf, fq)
    table_copy.wait()
    loads[5].wait()
    loads[6].wait()
    spread_forward(0, xf)
    consume_near(xf, acc_f)
    spread_start(1, xd, dq)
    consume_far(0, xf, acc_f, 0, 12)
    rep_start(0, acc_f, part_f, red_f)
    spread_forward(1, xd)

    s_one = rep_sum(0, acc_f, part_f, red_f).astype(BF16)
    pre_one = jnp.dot(s_one, w_one[...], preferred_element_type=F32)
    hidden, slope = gelu_parts(pre_one)
    hq[...] = hidden.astype(BF16)
    z_start(2, xh, hq)
    s_one_q[...] = s_one
    slope_q[...] = slope
    consume_near(xd, acc_d)
    spread_start(2, xh, hq)
    consume_far(1, xd, acc_d, 0, 12)
    rep_start(1, acc_d, part_d, red_d)
    spread_forward(2, xh)
    consume_near(xh, acc_h)
    d_pre = (rep_sum(1, acc_d, part_d, red_d) * slope_q[...]).astype(BF16)
    g_one = lax.dot_general(
        s_one_q[...], d_pre, (((0,), (0,)), ((), ())), preferred_element_type=F32
    )
    gpart[:, 0:8, :] = g_one.reshape(PLANE, 8, TILE)
    consume_far(2, xh, acc_h, 0, 12)
    rep_start(2, acc_h, part_h, red_h)

    g_two = lax.dot_general(
        part_h[...], cot[...], (((0,), (0,)), ((), ())), preferred_element_type=F32
    )
    gpart[:, 8:16, :] = g_two.reshape(PLANE, 8, TILE)

    def plane_sum(step):
        return remote(
            gpart.at[wrap(place + step, PLANE)], grs.at[step],
            g_send.at[0, step], g_recv.at[0, step], plane_peer(step),
        )

    def column_share(step):
        return remote(
            gcol.at[column], gcol.at[column],
            g_send.at[1, step], g_recv.at[1, step], column_peer(step),
        )

    def plane_gather(step):
        return remote(
            gred, gall.at[place],
            g_send.at[2, step], g_recv.at[2, step], plane_peer(step),
        )

    def start_all(make):
        def body(step, carry):
            make(step).start()
            return carry

        lax.fori_loop(1, PLANE, body, 0)

    def receive_all(make):
        def body(step, carry):
            make(step).wait_recv()
            return carry

        lax.fori_loop(1, PLANE, body, 0)

    def sent_all(make):
        def body(step, carry):
            make(step).wait_send()
            return carry

        lax.fori_loop(1, PLANE, body, 0)

    start_all(plane_sum)

    s_two = rep_sum(2, acc_h, part_h, red_h).astype(BF16)
    out_buf[quarter] = jnp.dot(s_two, w_two[...], preferred_element_type=F32).astype(BF16)

    def out_copy(step):
        return remote(
            out_buf.at[quarter], out_buf.at[quarter],
            o_send.at[step - 1], o_recv.at[step - 1], rep_peer(step),
        )

    for step in (2, 3, 1):
        out_copy(step).start()

    receive_all(plane_sum)
    mine = gpart[place]
    for step in range(1, PLANE):
        mine = mine + grs[step]
    gcol[column] = mine
    start_all(column_share)
    receive_all(column_share)
    mine = gcol[0]
    for other in range(1, PLANE):
        mine = mine + gcol[other]
    gred[...] = mine
    start_all(plane_gather)
    gall[place] = mine

    for step in (1, 2, 3):
        out_copy(step).wait_recv()
    out[...] = out_buf[...]
    receive_all(plane_gather)
    grad_one[...] = gall[:, 0:8, :].reshape(TILE, TILE)
    grad_two[...] = gall[:, 8:16, :].reshape(TILE, TILE)

    for t, buf, src in ((0, xf, fq), (1, xd, dq), (2, xh, hq)):
        z_finish(t, buf, src)
        spread_finish(t, buf)
    for t, part, red in ((0, part_f, red_f), (1, part_d, red_d), (2, part_h, red_h)):
        for step in (1, 2, 3):
            rep_copy(t, part, red, step).wait_send()
    for step in (1, 2, 3):
        out_copy(step).wait_send()
    sent_all(plane_sum)
    sent_all(column_share)
    sent_all(plane_gather)


def per_device(
    features, weight_one, weight_two, cotangent, adj_tiles, tile_rows, tile_cols, tile_counts
):
    vmem = pl.BlockSpec(memory_space=pltpu.VMEM)
    dma = pltpu.SemaphoreType.DMA
    return pl.pallas_call(
        step_kernel,
        name="graph_step",
        out_shape=(
            jax.ShapeDtypeStruct((NB, TILE), BF16),
            jax.ShapeDtypeStruct((TILE, TILE), F32),
            jax.ShapeDtypeStruct((TILE, TILE), F32),
        ),
        in_specs=[pl.BlockSpec(memory_space=pltpu.HBM)] * 8,
        out_specs=(vmem, vmem, vmem),
        scratch_shapes=[
            pltpu.VMEM((TILE, TILE), BF16),
            pltpu.VMEM((TILE, TILE), BF16),
            pltpu.VMEM((NB, TILE), BF16),
            pltpu.VMEM((PLANE, 16), jnp.int32),
            pltpu.VMEM((PLANE, 16), jnp.int32),
            pltpu.VMEM((1, 16), jnp.int32),
            pltpu.VMEM((DEAD + 1, TILE, TILE), BF16),
            pltpu.VMEM((PLANE, TILE), jnp.int32),
            pltpu.SMEM((PLANE, TILE), jnp.int32),
            pltpu.VMEM((PLANE, NB, TILE), BF16),
            pltpu.VMEM((PLANE, NB, TILE), BF16),
            pltpu.VMEM((PLANE, NB, TILE), BF16),
            pltpu.VMEM((TILE, TILE), BF16),
            pltpu.VMEM((TILE, TILE), BF16),
            pltpu.VMEM((NB, TILE), F32),
            pltpu.VMEM((NB, TILE), F32),
            pltpu.VMEM((NB, TILE), F32),
            pltpu.VMEM((NB, TILE), BF16),
            pltpu.VMEM((NB, TILE), BF16),
            pltpu.VMEM((NB, TILE), BF16),
            pltpu.VMEM((3, TILE, TILE), BF16),
            pltpu.VMEM((3, TILE, TILE), BF16),
            pltpu.VMEM((3, TILE, TILE), BF16),
            pltpu.VMEM((TILE, TILE), BF16),
            pltpu.VMEM((TILE, TILE), F32),
            pltpu.VMEM((NB, TILE), BF16),
            pltpu.VMEM((PLANE, 16, TILE), F32),
            pltpu.VMEM((PLANE, 16, TILE), F32),
            pltpu.VMEM((PLANE, 16, TILE), F32),
            pltpu.VMEM((16, TILE), F32),
            pltpu.VMEM((PLANE, 16, TILE), F32),
            dma((11,)),
            dma((3, 4)),
            dma((3, 4)),
            dma((3, 15)),
            dma((3, 15)),
            dma((3, 15)),
            dma((3, 15)),
            dma((3, 3)),
            dma((3, 3)),
            dma((3,)),
            dma((3,)),
            dma((3, 16)),
            dma((3, 16)),
        ],
        compiler_params=pltpu.CompilerParams(
            collective_id=0, has_side_effects=True, vmem_limit_bytes=64 << 20
        ),
    )(
        features, weight_one, weight_two, cotangent,
        adj_tiles.reshape(DEAD, TILE, TILE),
        tile_rows.reshape(PLANE, 16), tile_cols.reshape(PLANE, 16), tile_counts,
    )


def solution(mesh):
    placed = (
        P("row", None),
        P(),
        P(),
        P("row", None),
        P("row", "rep", None, None, None),
        P("row", "rep", None),
        P("row", "rep", None),
        P("row", "rep"),
    )
    return jax.shard_map(
        per_device,
        mesh=mesh,
        in_specs=placed,
        out_specs=(P("row", None), P(), P()),
        check_vma=False,
    )
```

```python
import jax
import jax.numpy as jnp
from jax import lax
from jax.experimental import pallas as pl
from jax.experimental.pallas import tpu as pltpu
from jax.sharding import PartitionSpec as P

MESH = pl.DeviceIdType.MESH
TILE = 128
NB = 512
HALF = 256
SIDE = 4
PLANE = 16
REPS = 4
DEAD = 256
BF16 = jnp.bfloat16
F32 = jnp.float32
GSUM = jnp.float32


def gelu_parts(values):
    normal_cdf = 0.5 * (1.0 + lax.erf(values * 0.7071067811865476))
    slope = normal_cdf + values * jnp.exp(-0.5 * values * values) * 0.3989422804014327
    return values * normal_cdf, slope


def wrap(value, size):
    return lax.rem(value + size, size)


def ring_step(index):
    return index + index // 2 - 2 * (index // 3)


def step_kernel(
    feat, w_one_in, w_two_in, cot_in, adj, rows_hbm, cols_hbm, counts_hbm,
    out, grads,
    w_one, w_two, cot, rows_in, cols_in, counts_in, tiles, table_v, table_s, xf, xd, xh, dq, hq, acc_f, acc_d, acc_h,
    part_f, part_d, part_h, red_f, red_d, red_h, s_one_q, slope_q, out_buf,
    gpart, grs, gcol, gred, gall,
    local_sem, z_send, z_recv, a_send, a_recv, b_send, b_recv,
    r_send, r_recv, o_send, o_recv, g_send, g_recv,
):
    row = lax.axis_index("row")
    rep = lax.axis_index("rep")
    zh = row // PLANE
    place = lax.rem(row, PLANE)
    y = place // SIDE
    x = lax.rem(place, SIDE)
    column = zh * REPS + rep


    def plane_peer(step):
        dy, dx = step // SIDE, lax.rem(step, SIDE)
        return (zh * PLANE + wrap(y + dy, SIDE) * SIDE + wrap(x + dx, SIDE), rep)

    def column_peer(step):
        dz, dc = step // 2, lax.rem(step, 2)
        z = lax.rem(2 * zh + rep // 2 + dz, 2 * REPS)
        return ((z // 2) * PLANE + place, lax.rem(z, 2) * 2 + lax.rem(rep + dc, 2))

    def rep_peer(step):
        return (row, wrap(rep + step, REPS))

    def x_peer(step):
        return (zh * PLANE + y * SIDE + wrap(x + step, SIDE), rep)

    def y_peer(step):
        return (zh * PLANE + wrap(y + step, SIDE) * SIDE + x, rep)

    def remote(src, dst, send, recv, peer):
        return pltpu.make_async_remote_copy(
            src_ref=src, dst_ref=dst, send_sem=send, recv_sem=recv,
            device_id=peer, device_id_type=MESH,
        )

    def local(src, dst, at):
        return pltpu.make_async_copy(src, dst, local_sem.at[at])

    barrier = pltpu.get_barrier_semaphore()

    def greet(peer):
        pl.semaphore_signal(barrier, inc=1, device_id=peer, device_id_type=MESH)

    for q in range(REPS):
        @pl.when(jnp.logical_or(rep != zh, rep != q))
        def _(q=q):
            greet((rep * PLANE + place, q))

    for step in (2, 1, 3):
        greet(x_peer(step))
        greet(y_peer(step))
        greet(rep_peer(step))
    loads = [
        local(cot_in, cot, 0), local(w_two_in, w_two, 1), local(counts_hbm, counts_in, 2),
        local(rows_hbm, rows_in, 3), local(cols_hbm, cols_in, 4), local(w_one_in, w_one, 5),
        local(adj, tiles.at[pl.ds(0, DEAD)], 6),
    ]
    for load in loads:
        load.start()
    pl.semaphore_wait(barrier, 13 - jnp.where(rep == zh, 1, 0))

    def z_copy(t, buf, src, step):
        return remote(
            src,
            buf.at[place, pl.ds(pl.multiple_of(rep * TILE, TILE), TILE)],
            z_send.at[t, step], z_recv.at[t, rep],
            (wrap(zh + step, REPS) * PLANE + place, zh),
        )

    def own_copy(t, buf, src):
        return local(src, buf.at[place, pl.ds(pl.multiple_of(rep * TILE, TILE), TILE)], 8 + t)

    def z_start(t, buf, src):
        for step in (2, 1, 3):
            z_copy(t, buf, src, step).start()

        @pl.when(rep != zh)
        def _():
            z_copy(t, buf, src, 0).start()

        @pl.when(rep == zh)
        def _():
            own_copy(t, buf, src).start()

    def z_finish(t, buf, src):
        for step in (1, 2, 3):
            z_copy(t, buf, src, step).wait_send()

        @pl.when(rep != zh)
        def _():
            z_copy(t, buf, src, 0).wait_send()

    def z_wait(t, buf, src, quarter):
        @pl.when(jnp.logical_or(rep != zh, rep != quarter))
        def _():
            remote(
                src, buf.at[place, pl.ds(quarter * TILE, TILE)],
                z_send.at[t, 0], z_recv.at[t, quarter], rep_peer(1),
            ).wait_recv()

        @pl.when(jnp.logical_and(rep == zh, rep == quarter))
        def _():
            own_copy(t, buf, src).wait()

    def a_block(dy, dx):
        return wrap(y - dy, SIDE) * SIDE + wrap(x - dx, SIDE)

    def half_a(buf, block):
        return buf.at[block, pl.ds(0, HALF)]

    def half_b(buf, block):
        return buf.at[block, pl.ds(HALF, HALF)]

    def first_a(t, buf, i, block):
        return remote(half_a(buf, block), half_a(buf, block),
                      a_send.at[t, i], a_recv.at[t, i], x_peer(ring_step(i + 1)))

    def first_b(t, buf, i, block):
        return remote(half_b(buf, block), half_b(buf, block),
                      b_send.at[t, i], b_recv.at[t, i], y_peer(ring_step(i + 1)))

    def second_a(t, buf, j, i, block):
        return remote(half_a(buf, block), half_a(buf, block),
                      a_send.at[t, 3 + 4 * j + i], a_recv.at[t, 3 + 4 * j + i],
                      y_peer(ring_step(j + 1)))

    def second_b(t, buf, j, i, block):
        return remote(half_b(buf, block), half_b(buf, block),
                      b_send.at[t, 3 + 4 * j + i], b_recv.at[t, 3 + 4 * j + i],
                      x_peer(ring_step(j + 1)))

    def spread_start(t, buf, src):
        z_wait(t, buf, src, 0)
        z_wait(t, buf, src, 1)
        for i in range(3):
            first_a(t, buf, i, place).start()
        z_wait(t, buf, src, 2)
        z_wait(t, buf, src, 3)
        for i in range(3):
            first_b(t, buf, i, place).start()
        for j in range(3):
            second_a(t, buf, j, 0, place).start()
            second_b(t, buf, j, 0, place).start()

    def spread_forward(t, buf):
        def body(i, carry):
            away = ring_step(i + 1)
            from_x = a_block(0, away)
            first_a(t, buf, i, from_x).wait_recv()
            for j in range(3):
                second_a(t, buf, j, i + 1, from_x).start()
            from_y = a_block(away, 0)
            first_b(t, buf, i, from_y).wait_recv()
            for j in range(3):
                second_b(t, buf, j, i + 1, from_y).start()
            return carry

        lax.fori_loop(0, 3, body, 0)

    def spread_finish(t, buf):
        def body(i, carry):
            first_a(t, buf, i, place).wait_send()
            first_b(t, buf, i, place).wait_send()
            for j in range(4):
                second_a(t, buf, i, j, place).wait_send()
                second_b(t, buf, i, j, place).wait_send()
            return carry

        lax.fori_loop(0, 3, body, 0)

    def multiply(acc, blocks, half, rights):
        right = jnp.concatenate(rights, axis=0)
        for k in range(4):
            left = jnp.concatenate(
                [tiles[table_s[block, 4 * k + 2 * half + c]] for block in blocks for c in range(2)],
                axis=1,
            )
            acc[pl.ds(k * TILE, TILE)] += jnp.dot(left, right, preferred_element_type=F32)

    def consume(buf, acc, blocks, half):
        multiply(acc, blocks, half, [buf[block, pl.ds(half * HALF, HALF)] for block in blocks])

    def consume_near(buf, acc):
        consume(buf, acc, [a_block(0, ring_step(i)) for i in range(4)], 0)
        consume(buf, acc, [a_block(ring_step(i), 0) for i in range(4)], 1)

    def consume_far(t, buf, acc, start, stop):
        def body(j, carry):
            e = ring_step(j + 1)
            blocks = [a_block(e, ring_step(i)) for i in range(4)]
            for i in range(4):
                second_a(t, buf, j, i, blocks[i]).wait_recv()
            consume(buf, acc, blocks, 0)
            blocks = [a_block(ring_step(i), e) for i in range(4)]
            for i in range(4):
                second_b(t, buf, j, i, blocks[i]).wait_recv()
            consume(buf, acc, blocks, 1)
            return carry

        lax.fori_loop(start // 4, stop // 4, body, 0)

    def rep_copy(t, part, red, step):
        return remote(
            part.at[pl.ds(pl.multiple_of(wrap(rep + step, REPS) * TILE, TILE), TILE)],
            red.at[step - 1], r_send.at[t, step - 1], r_recv.at[t, step - 1],
            rep_peer(step),
        )

    def rep_start(t, acc, part, red):
        part[...] = acc[...].astype(BF16)
        for step in (2, 3, 1):
            rep_copy(t, part, red, step).start()

    def rep_sum(t, acc, part, red):
        total = acc[pl.ds(pl.multiple_of(rep * TILE, TILE), TILE)]
        for step in (1, 2, 3):
            rep_copy(t, part, red, step).wait_recv()
            total = total + red[step - 1].astype(F32)
        return total

    quarter = pl.ds(pl.multiple_of(rep * TILE, TILE), TILE)

    fq = feat.at[quarter]
    z_start(0, xf, fq)
    loads[0].wait()
    loads[1].wait()
    dq[...] = lax.dot_general(
        cot[quarter], w_two[...], (((1,), (1,)), ((), ())), preferred_element_type=F32
    ).astype(BF16)

    loads[2].wait()
    loads[3].wait()
    loads[4].wait()
    lanes = lax.broadcasted_iota(jnp.int32, (PLANE, TILE), 1)
    sections = lax.broadcasted_iota(jnp.int32, (PLANE, TILE), 0)
    small_lane = lax.broadcasted_iota(jnp.int32, (PLANE, PLANE), 1)
    small_row = lax.broadcasted_iota(jnp.int32, (PLANE, PLANE), 0)
    count_wide = jnp.broadcast_to(counts_in[...].astype(F32), (PLANE, PLANE))
    count_col = jnp.sum(jnp.where(small_lane == small_row, count_wide, 0.0), axis=1, keepdims=True)
    cell = jnp.where(
        small_lane.astype(F32) < count_col, rows_in[...] * 4 + cols_in[...], -1
    )
    table = jnp.full((PLANE, TILE), DEAD, jnp.int32)
    for slot in range(16):
        table = jnp.where(cell[:, slot : slot + 1] == lanes, sections * 16 + slot, table)
    table_v[...] = table
    table_copy = local(table_v, table_s, 7)
    table_copy.start()
    tiles[DEAD] = jnp.zeros((TILE, TILE), BF16)
    acc_f[...] = jnp.zeros_like(acc_f)
    acc_d[...] = jnp.zeros_like(acc_d)
    acc_h[...] = jnp.zeros_like(acc_h)

    spread_start(0, xf, fq)
    z_start(1, xd, dq)
    table_copy.wait()
    loads[5].wait()
    loads[6].wait()
    spread_forward(0, xf)
    consume_near(xf, acc_f)
    spread_start(1, xd, dq)
    consume_far(0, xf, acc_f, 0, 12)
    rep_start(0, acc_f, part_f, red_f)
    spread_forward(1, xd)

    s_one = rep_sum(0, acc_f, part_f, red_f).astype(BF16)
    pre_one = jnp.dot(s_one, w_one[...], preferred_element_type=F32)
    hidden, slope = gelu_parts(pre_one)
    hq[...] = hidden.astype(BF16)
    z_start(2, xh, hq)
    s_one_q[...] = s_one
    slope_q[...] = slope
    consume_near(xd, acc_d)
    spread_start(2, xh, hq)
    consume_far(1, xd, acc_d, 0, 12)
    rep_start(1, acc_d, part_d, red_d)
    spread_forward(2, xh)
    consume_near(xh, acc_h)
    d_pre = (rep_sum(1, acc_d, part_d, red_d) * slope_q[...]).astype(BF16)
    g_one = lax.dot_general(
        s_one_q[...], d_pre, (((0,), (0,)), ((), ())), preferred_element_type=F32
    )
    gpart[:, 0:8, :] = g_one.reshape(PLANE, 8, TILE).astype(GSUM)
    consume_far(2, xh, acc_h, 0, 12)
    rep_start(2, acc_h, part_h, red_h)

    g_two = lax.dot_general(
        part_h[...], cot[...], (((0,), (0,)), ((), ())), preferred_element_type=F32
    )
    gpart[:, 8:16, :] = g_two.reshape(PLANE, 8, TILE).astype(GSUM)

    def plane_sum(step):
        return remote(
            gpart.at[lax.rem(plane_peer(step)[0], PLANE)], grs.at[step],
            g_send.at[0, step], g_recv.at[0, step], plane_peer(step),
        )

    def column_share(step):
        return remote(
            gcol.at[column], gcol.at[column],
            g_send.at[1, step], g_recv.at[1, step], column_peer(step),
        )

    def plane_gather(step):
        return remote(
            gred, gall.at[place],
            g_send.at[2, step], g_recv.at[2, step], plane_peer(step),
        )

    far_plane = (10, 6, 9, 11, 14, 2, 5, 7, 8, 13, 15, 1, 3, 4, 12)
    far_column = (8, 9, 6, 7, 10, 11, 4, 5, 12, 13, 2, 3, 14, 15, 1)

    def start_all(make, order):
        for step in order:
            make(step).start()

    def receive_all(make):
        for step in range(1, PLANE):
            make(step).wait_recv()

    def sent_all(make):
        def body(step, carry):
            make(step).wait_send()
            return carry

        lax.fori_loop(1, PLANE, body, 0)

    start_all(plane_sum, far_plane)

    s_two = rep_sum(2, acc_h, part_h, red_h).astype(BF16)
    out_buf[quarter] = jnp.dot(s_two, w_two[...], preferred_element_type=F32).astype(BF16)

    def out_copy(step):
        return remote(
            out_buf.at[quarter], out_buf.at[quarter],
            o_send.at[step - 1], o_recv.at[step - 1], rep_peer(step),
        )

    for step in (2, 3, 1):
        out_copy(step).start()

    receive_all(plane_sum)
    mine = gpart[place].astype(F32)
    for step in range(1, PLANE):
        mine = mine + grs[step].astype(F32)
    gcol[column] = mine.astype(GSUM)
    start_all(column_share, far_column)
    receive_all(column_share)
    mine = gcol[0].astype(F32)
    for other in range(1, PLANE):
        mine = mine + gcol[other].astype(F32)
    gred[...] = mine
    start_all(plane_gather, far_plane)
    gall[place] = mine

    for step in (1, 2, 3):
        out_copy(step).wait_recv()
    out[...] = out_buf[...]
    receive_all(plane_gather)
    grads[...] = gall[...]

    for t, buf, src in ((0, xf, fq), (1, xd, dq), (2, xh, hq)):
        z_finish(t, buf, src)
        spread_finish(t, buf)
    for t, part, red in ((0, part_f, red_f), (1, part_d, red_d), (2, part_h, red_h)):
        for step in (1, 2, 3):
            rep_copy(t, part, red, step).wait_send()
    for step in (1, 2, 3):
        out_copy(step).wait_send()
    sent_all(plane_sum)
    sent_all(column_share)
    sent_all(plane_gather)


def per_device(
    features, weight_one, weight_two, cotangent, adj_tiles, tile_rows, tile_cols, tile_counts
):
    vmem = pl.BlockSpec(memory_space=pltpu.VMEM)
    dma = pltpu.SemaphoreType.DMA
    output, grads = pl.pallas_call(
        step_kernel,
        name="graph_step",
        out_shape=(
            jax.ShapeDtypeStruct((NB, TILE), BF16),
            jax.ShapeDtypeStruct((PLANE, 16, TILE), F32),
        ),
        in_specs=[pl.BlockSpec(memory_space=pltpu.HBM)] * 8,
        out_specs=(vmem, vmem),
        scratch_shapes=[
            pltpu.VMEM((TILE, TILE), BF16),
            pltpu.VMEM((TILE, TILE), BF16),
            pltpu.VMEM((NB, TILE), BF16),
            pltpu.VMEM((PLANE, 16), jnp.int32),
            pltpu.VMEM((PLANE, 16), jnp.int32),
            pltpu.VMEM((1, 16), jnp.int32),
            pltpu.VMEM((DEAD + 1, TILE, TILE), BF16),
            pltpu.VMEM((PLANE, TILE), jnp.int32),
            pltpu.SMEM((PLANE, TILE), jnp.int32),
            pltpu.VMEM((PLANE, NB, TILE), BF16),
            pltpu.VMEM((PLANE, NB, TILE), BF16),
            pltpu.VMEM((PLANE, NB, TILE), BF16),
            pltpu.VMEM((TILE, TILE), BF16),
            pltpu.VMEM((TILE, TILE), BF16),
            pltpu.VMEM((NB, TILE), F32),
            pltpu.VMEM((NB, TILE), F32),
            pltpu.VMEM((NB, TILE), F32),
            pltpu.VMEM((NB, TILE), BF16),
            pltpu.VMEM((NB, TILE), BF16),
            pltpu.VMEM((NB, TILE), BF16),
            pltpu.VMEM((3, TILE, TILE), BF16),
            pltpu.VMEM((3, TILE, TILE), BF16),
            pltpu.VMEM((3, TILE, TILE), BF16),
            pltpu.VMEM((TILE, TILE), BF16),
            pltpu.VMEM((TILE, TILE), F32),
            pltpu.VMEM((NB, TILE), BF16),
            pltpu.VMEM((PLANE, 16, TILE), GSUM),
            pltpu.VMEM((PLANE, 16, TILE), GSUM),
            pltpu.VMEM((PLANE, 16, TILE), GSUM),
            pltpu.VMEM((16, TILE), F32),
            pltpu.VMEM((PLANE, 16, TILE), F32),
            dma((11,)),
            dma((3, 4)),
            dma((3, 4)),
            dma((3, 15)),
            dma((3, 15)),
            dma((3, 15)),
            dma((3, 15)),
            dma((3, 3)),
            dma((3, 3)),
            dma((3,)),
            dma((3,)),
            dma((3, 16)),
            dma((3, 16)),
        ],
        compiler_params=pltpu.CompilerParams(
            collective_id=0, has_side_effects=True, vmem_limit_bytes=64 << 20
        ),
    )(
        features, weight_one, weight_two, cotangent,
        adj_tiles.reshape(DEAD, TILE, TILE),
        tile_rows.reshape(PLANE, 16), tile_cols.reshape(PLANE, 16), tile_counts,
    )
    return (
        output,
        grads[:, 0:8, :].reshape(TILE, TILE),
        grads[:, 8:16, :].reshape(TILE, TILE),
    )


def solution(mesh):
    placed = (
        P("row", None),
        P(),
        P(),
        P("row", None),
        P("row", "rep", None, None, None),
        P("row", "rep", None),
        P("row", "rep", None),
        P("row", "rep"),
    )
    return jax.shard_map(
        per_device,
        mesh=mesh,
        in_specs=placed,
        out_specs=(P("row", None), P(), P()),
        check_vma=False,
    )
```

```python
import jax
import jax.numpy as jnp
from jax import lax
from jax.experimental import pallas as pl
from jax.experimental.pallas import tpu as pltpu
from jax.sharding import PartitionSpec as P

MESH = pl.DeviceIdType.MESH
TILE = 128
NB = 512
HALF = 256
SIDE = 4
PLANE = 16
REPS = 4
DEAD = 256
BF16 = jnp.bfloat16
F32 = jnp.float32
GSUM = jnp.float32


def gelu_parts(values):
    normal_cdf = 0.5 * (1.0 + lax.erf(values * 0.7071067811865476))
    slope = normal_cdf + values * jnp.exp(-0.5 * values * values) * 0.3989422804014327
    return values * normal_cdf, slope


def wrap(value, size):
    return lax.rem(value + size, size)


def ring_step(index):
    return index + index // 2 - 2 * (index // 3)


def step_kernel(
    feat, w_one_in, w_two_in, cot_in, adj, rows_hbm, cols_hbm, counts_hbm,
    out, grads,
    w_one, w_two, cot, rows_in, cols_in, counts_in, tiles, table_v, table_s, xf, xd, xh, dq, hq, acc_f, acc_d, acc_h,
    part_f, part_d, part_h, red_f, red_d, red_h, s_one_q, slope_q, out_buf,
    gpart, grs, gcol, gred, gall,
    local_sem, z_send, z_recv, a_send, a_recv, b_send, b_recv,
    r_send, r_recv, o_send, o_recv, g_send, g_recv,
):
    row = lax.axis_index("row")
    rep = lax.axis_index("rep")
    zh = row // PLANE
    place = lax.rem(row, PLANE)
    y = place // SIDE
    x = lax.rem(place, SIDE)
    column = zh * REPS + rep


    def plane_peer(step):
        dy, dx = step // SIDE, lax.rem(step, SIDE)
        return (zh * PLANE + wrap(y + dy, SIDE) * SIDE + wrap(x + dx, SIDE), rep)

    def column_peer(step):
        dz, dc = step // 2, lax.rem(step, 2)
        z = lax.rem(2 * zh + rep // 2 + dz, 2 * REPS)
        return ((z // 2) * PLANE + place, lax.rem(z, 2) * 2 + lax.rem(rep + dc, 2))

    def rep_peer(step):
        return (row, wrap(rep + step, REPS))

    def x_peer(step):
        return (zh * PLANE + y * SIDE + wrap(x + step, SIDE), rep)

    def y_peer(step):
        return (zh * PLANE + wrap(y + step, SIDE) * SIDE + x, rep)

    def remote(src, dst, send, recv, peer):
        return pltpu.make_async_remote_copy(
            src_ref=src, dst_ref=dst, send_sem=send, recv_sem=recv,
            device_id=peer, device_id_type=MESH,
        )

    def local(src, dst, at):
        return pltpu.make_async_copy(src, dst, local_sem.at[at])

    barrier = pltpu.get_barrier_semaphore()

    def greet(peer):
        pl.semaphore_signal(barrier, inc=1, device_id=peer, device_id_type=MESH)

    for q in range(REPS):
        @pl.when(jnp.logical_or(rep != zh, rep != q))
        def _(q=q):
            greet((rep * PLANE + place, q))

    for step in (2, 1, 3):
        greet(x_peer(step))
        greet(y_peer(step))
        greet(rep_peer(step))
    loads = [
        local(cot_in, cot, 0), local(w_two_in, w_two, 1), local(counts_hbm, counts_in, 2),
        local(rows_hbm, rows_in, 3), local(cols_hbm, cols_in, 4), local(w_one_in, w_one, 5),
        local(adj, tiles.at[pl.ds(0, DEAD)], 6),
    ]
    for load in loads:
        load.start()
    pl.semaphore_wait(barrier, 13 - jnp.where(rep == zh, 1, 0))

    def z_copy(t, buf, src, step):
        return remote(
            src,
            buf.at[place, pl.ds(pl.multiple_of(rep * TILE, TILE), TILE)],
            z_send.at[t, step], z_recv.at[t, rep],
            (wrap(zh + step, REPS) * PLANE + place, zh),
        )

    def own_copy(t, buf, src):
        return local(src, buf.at[place, pl.ds(pl.multiple_of(rep * TILE, TILE), TILE)], 8 + t)

    def z_start(t, buf, src):
        for step in (2, 1, 3):
            z_copy(t, buf, src, step).start()

        @pl.when(rep != zh)
        def _():
            z_copy(t, buf, src, 0).start()

        @pl.when(rep == zh)
        def _():
            own_copy(t, buf, src).start()

    def z_finish(t, buf, src):
        for step in (1, 2, 3):
            z_copy(t, buf, src, step).wait_send()

        @pl.when(rep != zh)
        def _():
            z_copy(t, buf, src, 0).wait_send()

    def z_wait(t, buf, src, quarter):
        @pl.when(jnp.logical_or(rep != zh, rep != quarter))
        def _():
            remote(
                src, buf.at[place, pl.ds(quarter * TILE, TILE)],
                z_send.at[t, 0], z_recv.at[t, quarter], rep_peer(1),
            ).wait_recv()

        @pl.when(jnp.logical_and(rep == zh, rep == quarter))
        def _():
            own_copy(t, buf, src).wait()

    def a_block(dy, dx):
        return wrap(y - dy, SIDE) * SIDE + wrap(x - dx, SIDE)

    def half_a(buf, block):
        return buf.at[block, pl.ds(0, HALF)]

    def half_b(buf, block):
        return buf.at[block, pl.ds(HALF, HALF)]

    def first_a(t, buf, i, block):
        return remote(half_a(buf, block), half_a(buf, block),
                      a_send.at[t, i], a_recv.at[t, i], x_peer(ring_step(i + 1)))

    def first_b(t, buf, i, block):
        return remote(half_b(buf, block), half_b(buf, block),
                      b_send.at[t, i], b_recv.at[t, i], y_peer(ring_step(i + 1)))

    def second_a(t, buf, j, i, block):
        return remote(half_a(buf, block), half_a(buf, block),
                      a_send.at[t, 3 + 4 * j + i], a_recv.at[t, 3 + 4 * j + i],
                      y_peer(ring_step(j + 1)))

    def second_b(t, buf, j, i, block):
        return remote(half_b(buf, block), half_b(buf, block),
                      b_send.at[t, 3 + 4 * j + i], b_recv.at[t, 3 + 4 * j + i],
                      x_peer(ring_step(j + 1)))

    def spread_start(t, buf, src):
        z_wait(t, buf, src, 0)
        z_wait(t, buf, src, 1)
        for i in range(3):
            first_a(t, buf, i, place).start()
        z_wait(t, buf, src, 2)
        z_wait(t, buf, src, 3)
        for i in range(3):
            first_b(t, buf, i, place).start()
        for j in range(3):
            second_a(t, buf, j, 0, place).start()
            second_b(t, buf, j, 0, place).start()

    def spread_forward(t, buf):
        def body(i, carry):
            away = ring_step(i + 1)
            from_x = a_block(0, away)
            first_a(t, buf, i, from_x).wait_recv()
            for j in range(3):
                second_a(t, buf, j, i + 1, from_x).start()
            from_y = a_block(away, 0)
            first_b(t, buf, i, from_y).wait_recv()
            for j in range(3):
                second_b(t, buf, j, i + 1, from_y).start()
            return carry

        lax.fori_loop(0, 3, body, 0)

    def spread_finish(t, buf):
        def body(i, carry):
            first_a(t, buf, i, place).wait_send()
            first_b(t, buf, i, place).wait_send()
            for j in range(4):
                second_a(t, buf, i, j, place).wait_send()
                second_b(t, buf, i, j, place).wait_send()
            return carry

        lax.fori_loop(0, 3, body, 0)

    def multiply(acc, blocks, half, rights):
        right = jnp.concatenate(rights, axis=0)
        for k in range(4):
            left = jnp.concatenate(
                [tiles[table_s[block, 4 * k + 2 * half + c]] for block in blocks for c in range(2)],
                axis=1,
            )
            acc[pl.ds(k * TILE, TILE)] += jnp.dot(left, right, preferred_element_type=F32)

    def consume(buf, acc, blocks, half):
        multiply(acc, blocks, half, [buf[block, pl.ds(half * HALF, HALF)] for block in blocks])

    def consume_near(buf, acc):
        consume(buf, acc, [a_block(0, ring_step(i)) for i in range(4)], 0)
        consume(buf, acc, [a_block(ring_step(i), 0) for i in range(4)], 1)

    def consume_far(t, buf, acc, start, stop):
        def body(j, carry):
            e = ring_step(j + 1)
            blocks = [a_block(e, ring_step(i)) for i in range(4)]
            for i in range(4):
                second_a(t, buf, j, i, blocks[i]).wait_recv()
            consume(buf, acc, blocks, 0)
            blocks = [a_block(ring_step(i), e) for i in range(4)]
            for i in range(4):
                second_b(t, buf, j, i, blocks[i]).wait_recv()
            consume(buf, acc, blocks, 1)
            return carry

        lax.fori_loop(start // 4, stop // 4, body, 0)

    def rep_copy(t, part, red, step):
        return remote(
            part.at[pl.ds(pl.multiple_of(wrap(rep + step, REPS) * TILE, TILE), TILE)],
            red.at[step - 1], r_send.at[t, step - 1], r_recv.at[t, step - 1],
            rep_peer(step),
        )

    def rep_start(t, acc, part, red):
        part[...] = acc[...].astype(BF16)
        for step in (2, 3, 1):
            rep_copy(t, part, red, step).start()

    def rep_sum(t, acc, part, red):
        total = acc[pl.ds(pl.multiple_of(rep * TILE, TILE), TILE)]
        for step in (1, 2, 3):
            rep_copy(t, part, red, step).wait_recv()
            total = total + red[step - 1].astype(F32)
        return total

    quarter = pl.ds(pl.multiple_of(rep * TILE, TILE), TILE)

    fq = feat.at[quarter]
    z_start(0, xf, fq)
    loads[0].wait()
    loads[1].wait()
    dq[...] = lax.dot_general(
        cot[quarter], w_two[...], (((1,), (1,)), ((), ())), preferred_element_type=F32
    ).astype(BF16)

    loads[2].wait()
    loads[3].wait()
    loads[4].wait()
    lanes = lax.broadcasted_iota(jnp.int32, (PLANE, TILE), 1)
    sections = lax.broadcasted_iota(jnp.int32, (PLANE, TILE), 0)
    small_lane = lax.broadcasted_iota(jnp.int32, (PLANE, PLANE), 1)
    small_row = lax.broadcasted_iota(jnp.int32, (PLANE, PLANE), 0)
    count_wide = jnp.broadcast_to(counts_in[...].astype(F32), (PLANE, PLANE))
    count_col = jnp.sum(jnp.where(small_lane == small_row, count_wide, 0.0), axis=1, keepdims=True)
    cell = jnp.where(
        small_lane.astype(F32) < count_col, rows_in[...] * 4 + cols_in[...], -1
    )
    table = jnp.full((PLANE, TILE), DEAD, jnp.int32)
    for slot in range(16):
        table = jnp.where(cell[:, slot : slot + 1] == lanes, sections * 16 + slot, table)
    table_v[...] = table
    table_copy = local(table_v, table_s, 7)
    table_copy.start()
    tiles[DEAD] = jnp.zeros((TILE, TILE), BF16)
    acc_f[...] = jnp.zeros_like(acc_f)
    acc_d[...] = jnp.zeros_like(acc_d)
    acc_h[...] = jnp.zeros_like(acc_h)

    spread_start(0, xf, fq)
    table_copy.wait()
    loads[5].wait()
    loads[6].wait()
    spread_forward(0, xf)
    z_start(1, xd, dq)
    consume_near(xf, acc_f)
    spread_start(1, xd, dq)
    consume_far(0, xf, acc_f, 0, 12)
    rep_start(0, acc_f, part_f, red_f)
    spread_forward(1, xd)

    s_one = rep_sum(0, acc_f, part_f, red_f).astype(BF16)
    pre_one = jnp.dot(s_one, w_one[...], preferred_element_type=F32)
    hidden, slope = gelu_parts(pre_one)
    hq[...] = hidden.astype(BF16)
    z_start(2, xh, hq)
    s_one_q[...] = s_one
    slope_q[...] = slope
    z_finish(0, xf, fq)
    spread_finish(0, xf)
    consume_near(xd, acc_d)
    spread_start(2, xh, hq)
    consume_far(1, xd, acc_d, 0, 12)
    rep_start(1, acc_d, part_d, red_d)
    spread_forward(2, xh)
    consume_near(xh, acc_h)
    d_pre = (rep_sum(1, acc_d, part_d, red_d) * slope_q[...]).astype(BF16)
    g_one = lax.dot_general(
        s_one_q[...], d_pre, (((0,), (0,)), ((), ())), preferred_element_type=F32
    )
    gpart[:, 0:8, :] = g_one.reshape(PLANE, 8, TILE).astype(GSUM)
    consume_far(2, xh, acc_h, 0, 12)
    rep_start(2, acc_h, part_h, red_h)

    g_two = lax.dot_general(
        part_h[...], cot[...], (((0,), (0,)), ((), ())), preferred_element_type=F32
    )
    gpart[:, 8:16, :] = g_two.reshape(PLANE, 8, TILE).astype(GSUM)

    def plane_sum(step):
        return remote(
            gpart.at[lax.rem(plane_peer(step)[0], PLANE)], grs.at[step],
            g_send.at[0, step], g_recv.at[0, step], plane_peer(step),
        )

    def column_share(step):
        return remote(
            gcol.at[column], gcol.at[column],
            g_send.at[1, step], g_recv.at[1, step], column_peer(step),
        )

    def plane_gather(step):
        return remote(
            gred, gall.at[place],
            g_send.at[2, step], g_recv.at[2, step], plane_peer(step),
        )

    far_plane = (10, 6, 9, 11, 14, 2, 5, 7, 8, 13, 15, 1, 3, 4, 12)
    far_column = (8, 9, 6, 7, 10, 11, 4, 5, 12, 13, 2, 3, 14, 15, 1)

    def start_all(make, order):
        for step in order:
            make(step).start()

    def receive_all(make):
        for step in range(1, PLANE):
            make(step).wait_recv()

    def sent_all(make):
        def body(step, carry):
            make(step).wait_send()
            return carry

        lax.fori_loop(1, PLANE, body, 0)

    start_all(plane_sum, far_plane)

    s_two = rep_sum(2, acc_h, part_h, red_h).astype(BF16)
    out_buf[quarter] = jnp.dot(s_two, w_two[...], preferred_element_type=F32).astype(BF16)

    def out_copy(step):
        return remote(
            out_buf.at[quarter], out_buf.at[quarter],
            o_send.at[step - 1], o_recv.at[step - 1], rep_peer(step),
        )

    for step in (2, 3, 1):
        out_copy(step).start()

    z_finish(1, xd, dq)
    spread_finish(1, xd)
    for t, part, red in ((0, part_f, red_f), (1, part_d, red_d)):
        for step in (1, 2, 3):
            rep_copy(t, part, red, step).wait_send()
    receive_all(plane_sum)
    mine = gpart[place].astype(F32)
    for step in range(1, PLANE):
        mine = mine + grs[step].astype(F32)
    gcol[column] = mine.astype(GSUM)
    start_all(column_share, far_column)
    z_finish(2, xh, hq)
    spread_finish(2, xh)
    for step in (1, 2, 3):
        rep_copy(2, part_h, red_h, step).wait_send()
    sent_all(plane_sum)
    receive_all(column_share)
    mine = gcol[0].astype(F32)
    for other in range(1, PLANE):
        mine = mine + gcol[other].astype(F32)
    gred[...] = mine
    start_all(plane_gather, far_plane)
    gall[place] = mine

    for step in (1, 2, 3):
        out_copy(step).wait_recv()
    out[...] = out_buf[...]
    for step in (1, 2, 3):
        out_copy(step).wait_send()
    sent_all(column_share)
    receive_all(plane_gather)
    grads[...] = gall[...]

    sent_all(plane_gather)


def per_device(
    features, weight_one, weight_two, cotangent, adj_tiles, tile_rows, tile_cols, tile_counts
):
    vmem = pl.BlockSpec(memory_space=pltpu.VMEM)
    dma = pltpu.SemaphoreType.DMA
    output, grads = pl.pallas_call(
        step_kernel,
        name="graph_step",
        out_shape=(
            jax.ShapeDtypeStruct((NB, TILE), BF16),
            jax.ShapeDtypeStruct((PLANE, 16, TILE), F32),
        ),
        in_specs=[pl.BlockSpec(memory_space=pltpu.HBM)] * 8,
        out_specs=(vmem, vmem),
        scratch_shapes=[
            pltpu.VMEM((TILE, TILE), BF16),
            pltpu.VMEM((TILE, TILE), BF16),
            pltpu.VMEM((NB, TILE), BF16),
            pltpu.VMEM((PLANE, 16), jnp.int32),
            pltpu.VMEM((PLANE, 16), jnp.int32),
            pltpu.VMEM((1, 16), jnp.int32),
            pltpu.VMEM((DEAD + 1, TILE, TILE), BF16),
            pltpu.VMEM((PLANE, TILE), jnp.int32),
            pltpu.SMEM((PLANE, TILE), jnp.int32),
            pltpu.VMEM((PLANE, NB, TILE), BF16),
            pltpu.VMEM((PLANE, NB, TILE), BF16),
            pltpu.VMEM((PLANE, NB, TILE), BF16),
            pltpu.VMEM((TILE, TILE), BF16),
            pltpu.VMEM((TILE, TILE), BF16),
            pltpu.VMEM((NB, TILE), F32),
            pltpu.VMEM((NB, TILE), F32),
            pltpu.VMEM((NB, TILE), F32),
            pltpu.VMEM((NB, TILE), BF16),
            pltpu.VMEM((NB, TILE), BF16),
            pltpu.VMEM((NB, TILE), BF16),
            pltpu.VMEM((3, TILE, TILE), BF16),
            pltpu.VMEM((3, TILE, TILE), BF16),
            pltpu.VMEM((3, TILE, TILE), BF16),
            pltpu.VMEM((TILE, TILE), BF16),
            pltpu.VMEM((TILE, TILE), F32),
            pltpu.VMEM((NB, TILE), BF16),
            pltpu.VMEM((PLANE, 16, TILE), GSUM),
            pltpu.VMEM((PLANE, 16, TILE), GSUM),
            pltpu.VMEM((PLANE, 16, TILE), GSUM),
            pltpu.VMEM((16, TILE), F32),
            pltpu.VMEM((PLANE, 16, TILE), F32),
            dma((11,)),
            dma((3, 4)),
            dma((3, 4)),
            dma((3, 15)),
            dma((3, 15)),
            dma((3, 15)),
            dma((3, 15)),
            dma((3, 3)),
            dma((3, 3)),
            dma((3,)),
            dma((3,)),
            dma((3, 16)),
            dma((3, 16)),
        ],
        compiler_params=pltpu.CompilerParams(
            collective_id=0, has_side_effects=True, vmem_limit_bytes=64 << 20
        ),
    )(
        features, weight_one, weight_two, cotangent,
        adj_tiles.reshape(DEAD, TILE, TILE),
        tile_rows.reshape(PLANE, 16), tile_cols.reshape(PLANE, 16), tile_counts,
    )
    return (
        output,
        grads[:, 0:8, :].reshape(TILE, TILE),
        grads[:, 8:16, :].reshape(TILE, TILE),
    )


def solution(mesh):
    placed = (
        P("row", None),
        P(),
        P(),
        P("row", None),
        P("row", "rep", None, None, None),
        P("row", "rep", None),
        P("row", "rep", None),
        P("row", "rep"),
    )
    return jax.shard_map(
        per_device,
        mesh=mesh,
        in_specs=placed,
        out_specs=(P("row", None), P(), P()),
        check_vma=False,
    )
```

```python
import jax
import jax.numpy as jnp
from jax import lax
from jax.experimental import pallas as pl
from jax.experimental.pallas import tpu as pltpu
from jax.sharding import PartitionSpec as P

MESH = pl.DeviceIdType.MESH
TILE = 128
NB = 512
HALF = 256
SIDE = 4
PLANE = 16
REPS = 4
DEAD = 256
BF16 = jnp.bfloat16
F32 = jnp.float32
GSUM = jnp.bfloat16


def gelu_parts(values):
    normal_cdf = 0.5 * (1.0 + lax.erf(values * 0.7071067811865476))
    slope = normal_cdf + values * jnp.exp(-0.5 * values * values) * 0.3989422804014327
    return values * normal_cdf, slope


def wrap(value, size):
    return lax.rem(value + size, size)


def ring_step(index):
    return index + index // 2 - 2 * (index // 3)


def step_kernel(
    feat, w_one_in, w_two_in, cot_in, adj, rows_hbm, cols_hbm, counts_hbm,
    out, grads,
    w_one, w_two, cot, rows_in, cols_in, counts_in, tiles, table_v, table_s, xf, xd, xh, dq, hq, acc_f, acc_d, acc_h,
    part_f, part_d, part_h, red_f, red_d, red_h, s_one_q, slope_q, out_buf,
    gpart, grs, gcol, gred, gall,
    local_sem, z_send, z_recv, a_send, a_recv, b_send, b_recv,
    r_send, r_recv, o_send, o_recv, g_send, g_recv,
):
    row = lax.axis_index("row")
    rep = lax.axis_index("rep")
    zh = row // PLANE
    place = lax.rem(row, PLANE)
    y = place // SIDE
    x = lax.rem(place, SIDE)
    column = zh * REPS + rep


    def plane_peer(step):
        dy, dx = step // SIDE, lax.rem(step, SIDE)
        return (zh * PLANE + wrap(y + dy, SIDE) * SIDE + wrap(x + dx, SIDE), rep)

    def column_peer(step):
        dz, dc = step // 2, lax.rem(step, 2)
        z = lax.rem(2 * zh + rep // 2 + dz, 2 * REPS)
        return ((z // 2) * PLANE + place, lax.rem(z, 2) * 2 + lax.rem(rep + dc, 2))

    def rep_peer(step):
        return (row, wrap(rep + step, REPS))

    def x_peer(step):
        return (zh * PLANE + y * SIDE + wrap(x + step, SIDE), rep)

    def y_peer(step):
        return (zh * PLANE + wrap(y + step, SIDE) * SIDE + x, rep)

    def remote(src, dst, send, recv, peer):
        return pltpu.make_async_remote_copy(
            src_ref=src, dst_ref=dst, send_sem=send, recv_sem=recv,
            device_id=peer, device_id_type=MESH,
        )

    def local(src, dst, at):
        return pltpu.make_async_copy(src, dst, local_sem.at[at])

    barrier = pltpu.get_barrier_semaphore()

    def greet(peer):
        pl.semaphore_signal(barrier, inc=1, device_id=peer, device_id_type=MESH)

    for q in range(REPS):
        @pl.when(jnp.logical_or(rep != zh, rep != q))
        def _(q=q):
            greet((rep * PLANE + place, q))

    for step in (2, 1, 3):
        greet(x_peer(step))
        greet(y_peer(step))
        greet(rep_peer(step))
    loads = [
        local(cot_in, cot, 0), local(w_two_in, w_two, 1), local(counts_hbm, counts_in, 2),
        local(rows_hbm, rows_in, 3), local(cols_hbm, cols_in, 4), local(w_one_in, w_one, 5),
        local(adj, tiles.at[pl.ds(0, DEAD)], 6),
    ]
    for load in loads:
        load.start()
    pl.semaphore_wait(barrier, 13 - jnp.where(rep == zh, 1, 0))

    def z_copy(t, buf, src, step):
        return remote(
            src,
            buf.at[place, pl.ds(pl.multiple_of(rep * TILE, TILE), TILE)],
            z_send.at[t, step], z_recv.at[t, rep],
            (wrap(zh + step, REPS) * PLANE + place, zh),
        )

    def own_copy(t, buf, src):
        return local(src, buf.at[place, pl.ds(pl.multiple_of(rep * TILE, TILE), TILE)], 8 + t)

    def z_start(t, buf, src):
        for step in (2, 1, 3):
            z_copy(t, buf, src, step).start()

        @pl.when(rep != zh)
        def _():
            z_copy(t, buf, src, 0).start()

        @pl.when(rep == zh)
        def _():
            own_copy(t, buf, src).start()

    def z_finish(t, buf, src):
        for step in (1, 2, 3):
            z_copy(t, buf, src, step).wait_send()

        @pl.when(rep != zh)
        def _():
            z_copy(t, buf, src, 0).wait_send()

    def z_wait(t, buf, src, quarter):
        @pl.when(jnp.logical_or(rep != zh, rep != quarter))
        def _():
            remote(
                src, buf.at[place, pl.ds(quarter * TILE, TILE)],
                z_send.at[t, 0], z_recv.at[t, quarter], rep_peer(1),
            ).wait_recv()

        @pl.when(jnp.logical_and(rep == zh, rep == quarter))
        def _():
            own_copy(t, buf, src).wait()

    def a_block(dy, dx):
        return wrap(y - dy, SIDE) * SIDE + wrap(x - dx, SIDE)

    def half_a(buf, block):
        return buf.at[block, pl.ds(0, HALF)]

    def half_b(buf, block):
        return buf.at[block, pl.ds(HALF, HALF)]

    def first_a(t, buf, i, block):
        return remote(half_a(buf, block), half_a(buf, block),
                      a_send.at[t, i], a_recv.at[t, i], x_peer(ring_step(i + 1)))

    def first_b(t, buf, i, block):
        return remote(half_b(buf, block), half_b(buf, block),
                      b_send.at[t, i], b_recv.at[t, i], y_peer(ring_step(i + 1)))

    def second_a(t, buf, j, i, block):
        return remote(half_a(buf, block), half_a(buf, block),
                      a_send.at[t, 3 + 4 * j + i], a_recv.at[t, 3 + 4 * j + i],
                      y_peer(ring_step(j + 1)))

    def second_b(t, buf, j, i, block):
        return remote(half_b(buf, block), half_b(buf, block),
                      b_send.at[t, 3 + 4 * j + i], b_recv.at[t, 3 + 4 * j + i],
                      x_peer(ring_step(j + 1)))

    def spread_start(t, buf, src):
        z_wait(t, buf, src, 0)
        z_wait(t, buf, src, 1)
        for i in range(3):
            first_a(t, buf, i, place).start()
        z_wait(t, buf, src, 2)
        z_wait(t, buf, src, 3)
        for i in range(3):
            first_b(t, buf, i, place).start()
        for j in range(3):
            second_a(t, buf, j, 0, place).start()
            second_b(t, buf, j, 0, place).start()

    def spread_forward(t, buf):
        def body(i, carry):
            away = ring_step(i + 1)
            from_x = a_block(0, away)
            first_a(t, buf, i, from_x).wait_recv()
            for j in range(3):
                second_a(t, buf, j, i + 1, from_x).start()
            from_y = a_block(away, 0)
            first_b(t, buf, i, from_y).wait_recv()
            for j in range(3):
                second_b(t, buf, j, i + 1, from_y).start()
            return carry

        lax.fori_loop(0, 3, body, 0)

    def spread_finish(t, buf):
        def body(i, carry):
            first_a(t, buf, i, place).wait_send()
            first_b(t, buf, i, place).wait_send()
            for j in range(4):
                second_a(t, buf, i, j, place).wait_send()
                second_b(t, buf, i, j, place).wait_send()
            return carry

        lax.fori_loop(0, 3, body, 0)

    def multiply(acc, blocks, half, rights):
        right = jnp.concatenate(rights, axis=0)
        for k in range(4):
            left = jnp.concatenate(
                [tiles[table_s[block, 4 * k + 2 * half + c]] for block in blocks for c in range(2)],
                axis=1,
            )
            acc[pl.ds(k * TILE, TILE)] += jnp.dot(left, right, preferred_element_type=F32)

    def consume(buf, acc, blocks, half):
        multiply(acc, blocks, half, [buf[block, pl.ds(half * HALF, HALF)] for block in blocks])

    def consume_near(buf, acc):
        consume(buf, acc, [a_block(0, ring_step(i)) for i in range(4)], 0)
        consume(buf, acc, [a_block(ring_step(i), 0) for i in range(4)], 1)

    def consume_far(t, buf, acc, start, stop):
        def body(j, carry):
            e = ring_step(j + 1)
            blocks = [a_block(e, ring_step(i)) for i in range(4)]
            for i in range(4):
                second_a(t, buf, j, i, blocks[i]).wait_recv()
            consume(buf, acc, blocks, 0)
            blocks = [a_block(ring_step(i), e) for i in range(4)]
            for i in range(4):
                second_b(t, buf, j, i, blocks[i]).wait_recv()
            consume(buf, acc, blocks, 1)
            return carry

        lax.fori_loop(start // 4, stop // 4, body, 0)

    def rep_copy(t, part, red, step):
        return remote(
            part.at[pl.ds(pl.multiple_of(wrap(rep + step, REPS) * TILE, TILE), TILE)],
            red.at[step - 1], r_send.at[t, step - 1], r_recv.at[t, step - 1],
            rep_peer(step),
        )

    def rep_start(t, acc, part, red):
        part[...] = acc[...].astype(BF16)
        for step in (2, 3, 1):
            rep_copy(t, part, red, step).start()

    def rep_sum(t, acc, part, red):
        total = acc[pl.ds(pl.multiple_of(rep * TILE, TILE), TILE)]
        for step in (1, 2, 3):
            rep_copy(t, part, red, step).wait_recv()
            total = total + red[step - 1].astype(F32)
        return total

    quarter = pl.ds(pl.multiple_of(rep * TILE, TILE), TILE)

    fq = feat.at[quarter]
    z_start(0, xf, fq)
    loads[0].wait()
    loads[1].wait()
    dq[...] = lax.dot_general(
        cot[quarter], w_two[...], (((1,), (1,)), ((), ())), preferred_element_type=F32
    ).astype(BF16)

    loads[2].wait()
    loads[3].wait()
    loads[4].wait()
    lanes = lax.broadcasted_iota(jnp.int32, (PLANE, TILE), 1)
    sections = lax.broadcasted_iota(jnp.int32, (PLANE, TILE), 0)
    small_lane = lax.broadcasted_iota(jnp.int32, (PLANE, PLANE), 1)
    small_row = lax.broadcasted_iota(jnp.int32, (PLANE, PLANE), 0)
    count_wide = jnp.broadcast_to(counts_in[...].astype(F32), (PLANE, PLANE))
    count_col = jnp.sum(jnp.where(small_lane == small_row, count_wide, 0.0), axis=1, keepdims=True)
    cell = jnp.where(
        small_lane.astype(F32) < count_col, rows_in[...] * 4 + cols_in[...], -1
    )
    table = jnp.full((PLANE, TILE), DEAD, jnp.int32)
    for slot in range(16):
        table = jnp.where(cell[:, slot : slot + 1] == lanes, sections * 16 + slot, table)
    table_v[...] = table
    table_copy = local(table_v, table_s, 7)
    table_copy.start()
    tiles[DEAD] = jnp.zeros((TILE, TILE), BF16)
    acc_f[...] = jnp.zeros_like(acc_f)
    acc_d[...] = jnp.zeros_like(acc_d)
    acc_h[...] = jnp.zeros_like(acc_h)

    spread_start(0, xf, fq)
    table_copy.wait()
    loads[5].wait()
    loads[6].wait()
    spread_forward(0, xf)
    z_start(1, xd, dq)
    consume_near(xf, acc_f)
    spread_start(1, xd, dq)
    consume_far(0, xf, acc_f, 0, 12)
    rep_start(0, acc_f, part_f, red_f)
    spread_forward(1, xd)

    s_one = rep_sum(0, acc_f, part_f, red_f).astype(BF16)
    pre_one = jnp.dot(s_one, w_one[...], preferred_element_type=F32)
    hidden, slope = gelu_parts(pre_one)
    hq[...] = hidden.astype(BF16)
    z_start(2, xh, hq)
    s_one_q[...] = s_one
    slope_q[...] = slope
    z_finish(0, xf, fq)
    spread_finish(0, xf)
    consume_near(xd, acc_d)
    spread_start(2, xh, hq)
    consume_far(1, xd, acc_d, 0, 12)
    rep_start(1, acc_d, part_d, red_d)
    spread_forward(2, xh)
    consume_near(xh, acc_h)
    d_pre = (rep_sum(1, acc_d, part_d, red_d) * slope_q[...]).astype(BF16)
    g_one = lax.dot_general(
        s_one_q[...], d_pre, (((0,), (0,)), ((), ())), preferred_element_type=F32
    )
    gpart[:, 0:8, :] = g_one.reshape(PLANE, 8, TILE).astype(GSUM)
    consume_far(2, xh, acc_h, 0, 12)
    rep_start(2, acc_h, part_h, red_h)

    g_two = lax.dot_general(
        part_h[...], cot[...], (((0,), (0,)), ((), ())), preferred_element_type=F32
    )
    gpart[:, 8:16, :] = g_two.reshape(PLANE, 8, TILE).astype(GSUM)

    def plane_sum(step):
        return remote(
            gpart.at[lax.rem(plane_peer(step)[0], PLANE)], grs.at[step],
            g_send.at[0, step], g_recv.at[0, step], plane_peer(step),
        )

    def column_share(step):
        return remote(
            gcol.at[column], gcol.at[column],
            g_send.at[1, step], g_recv.at[1, step], column_peer(step),
        )

    def plane_gather(step):
        return remote(
            gred, gall.at[place],
            g_send.at[2, step], g_recv.at[2, step], plane_peer(step),
        )

    far_plane = (10, 6, 9, 11, 14, 2, 5, 7, 8, 13, 15, 1, 3, 4, 12)
    far_column = (8, 9, 6, 7, 10, 11, 4, 5, 12, 13, 2, 3, 14, 15, 1)

    def start_all(make, order):
        for step in order:
            make(step).start()

    def receive_all(make):
        for step in range(1, PLANE):
            make(step).wait_recv()

    def sent_all(make):
        def body(step, carry):
            make(step).wait_send()
            return carry

        lax.fori_loop(1, PLANE, body, 0)

    start_all(plane_sum, far_plane)

    s_two = rep_sum(2, acc_h, part_h, red_h).astype(BF16)
    out_buf[quarter] = jnp.dot(s_two, w_two[...], preferred_element_type=F32).astype(BF16)

    def out_copy(step):
        return remote(
            out_buf.at[quarter], out_buf.at[quarter],
            o_send.at[step - 1], o_recv.at[step - 1], rep_peer(step),
        )

    for step in (2, 3, 1):
        out_copy(step).start()

    z_finish(1, xd, dq)
    spread_finish(1, xd)
    for t, part, red in ((0, part_f, red_f), (1, part_d, red_d)):
        for step in (1, 2, 3):
            rep_copy(t, part, red, step).wait_send()
    receive_all(plane_sum)
    mine = gpart[place].astype(F32)
    for step in range(1, PLANE):
        mine = mine + grs[step].astype(F32)
    gcol[column] = mine.astype(GSUM)
    start_all(column_share, far_column)
    z_finish(2, xh, hq)
    spread_finish(2, xh)
    for step in (1, 2, 3):
        rep_copy(2, part_h, red_h, step).wait_send()
    sent_all(plane_sum)
    receive_all(column_share)
    mine = gcol[0].astype(F32)
    for other in range(1, PLANE):
        mine = mine + gcol[other].astype(F32)
    gred[...] = mine
    start_all(plane_gather, far_plane)
    gall[place] = mine

    for step in (1, 2, 3):
        out_copy(step).wait_recv()
    out[...] = out_buf[...]
    for step in (1, 2, 3):
        out_copy(step).wait_send()
    sent_all(column_share)
    receive_all(plane_gather)
    grads[...] = gall[...]

    sent_all(plane_gather)


def per_device(
    features, weight_one, weight_two, cotangent, adj_tiles, tile_rows, tile_cols, tile_counts
):
    vmem = pl.BlockSpec(memory_space=pltpu.VMEM)
    dma = pltpu.SemaphoreType.DMA
    output, grads = pl.pallas_call(
        step_kernel,
        name="graph_step",
        out_shape=(
            jax.ShapeDtypeStruct((NB, TILE), BF16),
            jax.ShapeDtypeStruct((PLANE, 16, TILE), F32),
        ),
        in_specs=[pl.BlockSpec(memory_space=pltpu.HBM)] * 8,
        out_specs=(vmem, vmem),
        scratch_shapes=[
            pltpu.VMEM((TILE, TILE), BF16),
            pltpu.VMEM((TILE, TILE), BF16),
            pltpu.VMEM((NB, TILE), BF16),
            pltpu.VMEM((PLANE, 16), jnp.int32),
            pltpu.VMEM((PLANE, 16), jnp.int32),
            pltpu.VMEM((1, 16), jnp.int32),
            pltpu.VMEM((DEAD + 1, TILE, TILE), BF16),
            pltpu.VMEM((PLANE, TILE), jnp.int32),
            pltpu.SMEM((PLANE, TILE), jnp.int32),
            pltpu.VMEM((PLANE, NB, TILE), BF16),
            pltpu.VMEM((PLANE, NB, TILE), BF16),
            pltpu.VMEM((PLANE, NB, TILE), BF16),
            pltpu.VMEM((TILE, TILE), BF16),
            pltpu.VMEM((TILE, TILE), BF16),
            pltpu.VMEM((NB, TILE), F32),
            pltpu.VMEM((NB, TILE), F32),
            pltpu.VMEM((NB, TILE), F32),
            pltpu.VMEM((NB, TILE), BF16),
            pltpu.VMEM((NB, TILE), BF16),
            pltpu.VMEM((NB, TILE), BF16),
            pltpu.VMEM((3, TILE, TILE), BF16),
            pltpu.VMEM((3, TILE, TILE), BF16),
            pltpu.VMEM((3, TILE, TILE), BF16),
            pltpu.VMEM((TILE, TILE), BF16),
            pltpu.VMEM((TILE, TILE), F32),
            pltpu.VMEM((NB, TILE), BF16),
            pltpu.VMEM((PLANE, 16, TILE), GSUM),
            pltpu.VMEM((PLANE, 16, TILE), GSUM),
            pltpu.VMEM((PLANE, 16, TILE), GSUM),
            pltpu.VMEM((16, TILE), F32),
            pltpu.VMEM((PLANE, 16, TILE), F32),
            dma((11,)),
            dma((3, 4)),
            dma((3, 4)),
            dma((3, 15)),
            dma((3, 15)),
            dma((3, 15)),
            dma((3, 15)),
            dma((3, 3)),
            dma((3, 3)),
            dma((3,)),
            dma((3,)),
            dma((3, 16)),
            dma((3, 16)),
        ],
        compiler_params=pltpu.CompilerParams(
            collective_id=0, has_side_effects=True, vmem_limit_bytes=64 << 20
        ),
    )(
        features, weight_one, weight_two, cotangent,
        adj_tiles.reshape(DEAD, TILE, TILE),
        tile_rows.reshape(PLANE, 16), tile_cols.reshape(PLANE, 16), tile_counts,
    )
    return (
        output,
        grads[:, 0:8, :].reshape(TILE, TILE),
        grads[:, 8:16, :].reshape(TILE, TILE),
    )


def solution(mesh):
    placed = (
        P("row", None),
        P(),
        P(),
        P("row", None),
        P("row", "rep", None, None, None),
        P("row", "rep", None),
        P("row", "rep", None),
        P("row", "rep"),
    )
    return jax.shard_map(
        per_device,
        mesh=mesh,
        in_specs=placed,
        out_specs=(P("row", None), P(), P()),
        check_vma=False,
    )
```
